32 devices in a mesh: groups: 2 (over y), seq: 16 (over z, x, core).
Axes of the slice: x: 2, y: 2, z: 4, core: 2. Of those that a mesh axis runs over, the one named last changes fastest.
Arguments:
- xbc: bfloat16 [16384, 2304], P(('groups', 'seq')), parts along dimension 0, may hold values from -24 to 24
- conv_weight: float32 [4, 2304], replicated, may hold values from -3 to 3
- log_decay: float32 [16, 16384], P(None, ('groups', 'seq')), parts along dimension 1, may hold values from -1 to 0, as said below
- level_weights: float32 [16, 14, 16384], P(None, None, ('groups', 'seq')), parts along dimension 2, may hold values from 0.1 to 1
- gain: float32 [2048], replicated, may hold values from 0.25 to 1.75
Outputs:
- mixed: bfloat16 [16384, 2048], P(('groups', 'seq')), parts along dimension 0
The draws below stay inside these ranges and needn't reach their ends.
There are 2 independent parts, one for each index of `groups`. The reference program is written for one: setup_inputs(seed, part) draws one part's arguments, and reference() takes and returns one part's arrays. A program takes and returns all parts, laid end to end along the dimension named above; an argument that names none is the same for every part. Nothing has to cross between parts.
Inputs may be any that keep to these rules, and one draw needn't show every extreme that they name: `log_decay`: every entry is negative.
All inputs are finite; a program needn't handle non-finite values.
Results may differ from the reference program's by a relative error of at most 0.0034.
Values may be sent and summed in bfloat16 or wider, within the bound.
A program may use at most 128 MiB of HBM per device.

```python
import math
import jax
import jax.numpy as jnp
from jax import lax

PAIRED_MIXER_NUM = 16
HEAD_DIM = 128
STATE = 128
KERNEL = 4
TOK_DEV = 512
INNER = 2048
WIDTH = 2304
STEP_AMOUNT = 8192
LOG_TOK = 9
LOG_SEQ = 4
LEVELS = 14


def draw_xbc(key, part):
    key_base, key_cols, key_rows = jax.random.split(key, 3)
    col_scale = jnp.exp(jax.random.uniform(key_cols, (1, WIDTH), jnp.float32, math.log(0.4), math.log(4.0)))
    row_scale = jnp.exp(jax.random.uniform(key_rows, (STEP_AMOUNT, 1), jnp.float32, math.log(0.5), math.log(2.0)))
    entries = jax.random.normal(key_base, (STEP_AMOUNT, WIDTH), jnp.float32) * col_scale * row_scale
    return jnp.clip(entries, -24.0, 24.0).astype(jnp.bfloat16)


def draw_log_decay(key, part):
    lookup_vectors = jax.random.split(key, 9)
    head_kind = jax.random.randint(lookup_vectors[0], (PAIRED_MIXER_NUM, 1), 0, 4)
    fast_rate = jnp.exp(jax.random.uniform(lookup_vectors[2], (PAIRED_MIXER_NUM, 1), jnp.float32, math.log(1.0 / 50.0), math.log(1.0 / 30.0)))
    medium_rate = jnp.exp(jax.random.uniform(lookup_vectors[3], (PAIRED_MIXER_NUM, 1), jnp.float32, math.log(0.5), math.log(2.0))) / TOK_DEV
    slow_rate = jnp.exp(jax.random.uniform(lookup_vectors[4], (PAIRED_MIXER_NUM, 1), jnp.float32, math.log(0.1), math.log(0.4))) / STEP_AMOUNT
    channel_forget_factor = jnp.where(head_kind == 0, fast_rate, jnp.where(head_kind == 1, medium_rate, slow_rate))
    segment_factor = jnp.exp(jax.random.uniform(lookup_vectors[5], (PAIRED_MIXER_NUM, STEP_AMOUNT // TOK_DEV), jnp.float32, math.log(0.5), math.log(2.0)))
    segment_factor = jnp.repeat(segment_factor, TOK_DEV, axis=1)
    element_factor = jnp.exp(jax.random.uniform(lookup_vectors[6], (PAIRED_MIXER_NUM, STEP_AMOUNT), jnp.float32, math.log(0.5), math.log(2.0)))
    segment_offset = jax.random.randint(lookup_vectors[7], (PAIRED_MIXER_NUM, 3, 1), 0, STEP_AMOUNT)
    segment_size = jax.random.uniform(lookup_vectors[8], (PAIRED_MIXER_NUM, 3, 1), jnp.float32, 0.22, 0.5)
    element_index = lax.iota(jnp.int32, STEP_AMOUNT)[None, None, :]
    segment_list = jnp.sum(jnp.where(element_index == segment_offset, segment_size, 0.0), axis=1)
    return -(channel_forget_factor * segment_factor * element_factor + segment_list)


def steps_of(key, shape, cuts, least, largest):
    loudness, own = 1.0, jax.random.fold_in(key, 6)
    for dim, parts in cuts:
        heights = jnp.exp(jax.random.uniform(jax.random.fold_in(own, dim), (parts,), jnp.float32, least / len(cuts), largest / len(cuts)))
        loudness = loudness * jnp.repeat(heights, shape[dim] // parts).reshape([-1 if axis == dim else 1 for axis in range(len(shape))])
    return loudness


def gaussian(rng, extent, spread, most, held_as=jnp.bfloat16):
    drawn = jax.random.normal(rng, extent, jnp.float32) * spread
    return jnp.minimum(jnp.maximum(drawn, -most), most).astype(held_as)


def setup_inputs(seed: int = 0, part: int = 0) -> dict:
    keys = jax.random.split(jax.random.key(seed), 6)
    own_keys = jax.random.split(jax.random.fold_in(keys[5], part), 6)
    return {
        "xbc": draw_xbc(jax.random.fold_in(jax.random.fold_in(keys[5], part), 71), part),
        "conv_weight": gaussian(keys[1], (KERNEL, WIDTH), KERNEL ** -0.5, 3.0, jnp.float32),
        "log_decay": draw_log_decay(jax.random.fold_in(jax.random.fold_in(keys[5], part), 71), part),
        "level_weights": jnp.clip(jnp.exp(math.log(1.0) - 2.3025851 * jax.random.uniform(own_keys[3], (PAIRED_MIXER_NUM, LEVELS, STEP_AMOUNT), jnp.float32) ** steps_of(own_keys[3], (PAIRED_MIXER_NUM, LEVELS, STEP_AMOUNT), ((2, 16),), -0.2, 0.2)), 0.1, 1.0),
        "gain": jnp.clip(1.0 + 0.15 * jax.random.normal(keys[4], (INNER,), jnp.float32), 0.25, 1.75),
    }


def bit_length(numbers, limit):
    counted = jnp.zeros(numbers.shape, jnp.int32)
    for power_index in range(limit):
        counted = counted + (numbers >= 1 << power_index).astype(jnp.int32)
    return counted

def compute_near(values_rows, in_map, out_map, local_log, level_gain, head_count):
    row_count = values_rows.shape[0]
    head_dim = values_rows.shape[1] // head_count
    local_bits = row_count.bit_length() - 1
    scores = jnp.dot(out_map, in_map.T, preferred_element_type=jnp.float32)
    element_index = lax.iota(jnp.int32, row_count)
    level_index = bit_length(jnp.bitwise_xor(element_index[:, None], element_index[None, :]), local_bits)
    causal = element_index[None, :] <= element_index[:, None]
    chosen = jnp.zeros((head_count, row_count, row_count), jnp.float32)
    for level_step in range(local_bits + 1):
        chosen = jnp.where((level_index == level_step)[None], level_gain[:, level_step, :, None], chosen)
    gap_log = jnp.where(causal[None], local_log[:, :, None] - local_log[:, None, :], -1e+30)
    weight = (chosen * jnp.exp(gap_log) * scores[None]).astype(jnp.bfloat16)
    shaped = values_rows.reshape(row_count, head_count, head_dim).astype(jnp.float32)
    near_heads = jnp.einsum('hts,shp->thp', weight.astype(jnp.float32), shaped)
    return near_heads.reshape(row_count, head_count * head_dim)

def reference(xbc, conv_weight, log_decay, level_weights, gain):
    inner_width = PAIRED_MIXER_NUM * HEAD_DIM
    blocks = STEP_AMOUNT // TOK_DEV
    padded = jnp.concatenate([jnp.zeros((KERNEL - 1, xbc.shape[1]), jnp.float32), xbc.astype(jnp.float32)], axis=0)
    convolved = padded[0:STEP_AMOUNT] * conv_weight[0]
    for offset in range(1, KERNEL):
        convolved = convolved + padded[offset:offset + STEP_AMOUNT] * conv_weight[offset]
    activated = jax.nn.silu(convolved).astype(jnp.bfloat16)
    values_all = activated[:, :inner_width].reshape(blocks, TOK_DEV, inner_width)
    in_all = activated[:, inner_width:inner_width + STATE].reshape(blocks, TOK_DEV, STATE)
    out_all = activated[:, inner_width + STATE:].reshape(blocks, TOK_DEV, STATE)
    local_log = jnp.cumsum(log_decay.reshape(PAIRED_MIXER_NUM, blocks, TOK_DEV), axis=2)
    block_total = local_log[:, :, TOK_DEV - 1]
    inclusive = jnp.cumsum(block_total, axis=1)
    before = inclusive - block_total

    def state_of(pieces):
        values_block, in_block, log_block, total_block = pieces
        tail_decay = jnp.exp(total_block[:, None] - log_block)
        decayed = (values_block.reshape(TOK_DEV, PAIRED_MIXER_NUM, HEAD_DIM) * tail_decay.T[:, :, None]).reshape(TOK_DEV, inner_width).astype(jnp.bfloat16)
        return jnp.dot(in_block.T, decayed, preferred_element_type=jnp.float32)
    states = lax.map(state_of, (values_all, in_all, local_log.transpose(1, 0, 2), block_total.T))
    group_list = []
    for level_index in range(1, LOG_SEQ + 1):
        group_span = 2 ** (level_index - 1)
        group_count = blocks // group_span
        grouped = states.reshape(group_count, group_span, STATE, PAIRED_MIXER_NUM, HEAD_DIM)
        ends_log = inclusive.reshape(PAIRED_MIXER_NUM, group_count, group_span)
        weight = jnp.exp(ends_log[:, :, group_span - 1:group_span] - ends_log)
        level_node = jnp.einsum('hgm,gmnhp->gnhp', weight, grouped, precision=lax.Precision.HIGHEST)
        group_list.append((level_node.reshape(group_count, STATE, inner_width), ends_log[:, :, group_span - 1]))

    def output_of(pieces):
        block_index, values_block, in_block, out_block, log_block, gain_block, start_log = pieces
        near_term = compute_near(values_block, in_block, out_block, log_block, gain_block, PAIRED_MIXER_NUM)
        far_term = jnp.zeros((TOK_DEV, inner_width), jnp.float32)
        queries_wide = out_block.astype(jnp.float32)
        for level_index in range(1, LOG_SEQ + 1):
            node_all, group_ends = group_list[level_index - 1]
            is_upper = block_index >> level_index - 1 & 1 == 1
            group_slot = jnp.maximum((block_index >> level_index - 1) - 1, 0).astype(jnp.int32)
            level_node = node_all[group_slot]
            gap_log = start_log - group_ends[:, group_slot]
            exponent = jnp.where(is_upper, log_block + gap_log[:, None], -1e+30)
            factor = gain_block[:, LOG_TOK + level_index, :] * jnp.exp(exponent)
            product = jnp.dot(queries_wide, level_node, precision=lax.Precision.HIGHEST)
            far_term = far_term + (product.reshape(TOK_DEV, PAIRED_MIXER_NUM, HEAD_DIM) * factor.T[:, :, None]).reshape(TOK_DEV, inner_width)
        mixed_sum = (near_term + far_term).reshape(TOK_DEV, PAIRED_MIXER_NUM, HEAD_DIM)
        inv_rms = lax.rsqrt(lax.optimization_barrier(jnp.mean(mixed_sum * mixed_sum, axis=2, keepdims=True)) + 1e-05)
        return ((mixed_sum * inv_rms).reshape(TOK_DEV, inner_width) * gain).astype(jnp.bfloat16)
    gains_blocks = level_weights.reshape(PAIRED_MIXER_NUM, LEVELS, blocks, TOK_DEV).transpose(2, 0, 1, 3)
    result = lax.map(output_of, (jnp.arange(blocks, dtype=jnp.int32), values_all, in_all, out_all, local_log.transpose(1, 0, 2), gains_blocks, before.T))
    return result.reshape(STEP_AMOUNT, inner_width)
```

```python
import functools
import jax
import jax.numpy as jnp
from jax import lax
from jax.experimental import pallas as pl
from jax.experimental.pallas import tpu as pltpu
from jax.sharding import PartitionSpec as P

LANES = 128
PACK = 16
MESH = pl.DeviceIdType.MESH
F32, BF16 = jnp.float32, jnp.bfloat16


def lane(i, width=LANES):
    if isinstance(i, int):
        return pl.ds(i * width, width)
    return pl.ds(pl.multiple_of(i * width, LANES), width)


def packed(row, times=1):
    return jnp.broadcast_to(row, (PACK * times, row.shape[1])).astype(BF16)


def kernel(
    seq_bits, xbc_hbm, taps_hbm, decay_hbm, lw_hbm, gain_hbm, out,
    xbc, taps, decay, lw, gain, load_sem, pad, edge, halo, vbuf, out_map_t, values_t, dec,
    tail, col, diag, cross, far_row, scores_t, wt, fw, near_t, gain_col,
    agg, send, node, span, span_rx, prefix,
    halo_sem, span_send, span_recv, chip_send, chip_recv, step_send, step_recv, xf_send, xf_recv, cf_send, cf_recv,
):
    rows, width = xbc.shape
    heads = decay.shape[0]
    kern = taps.shape[0]
    half = heads // 2
    CH = 4
    per = half // CH
    tiles = rows // LANES
    tile_bits = LANES.bit_length() - 1
    local_bits = rows.bit_length() - 1
    count = 1 << seq_bits
    last = seq_bits - 1
    me = lax.axis_index("seq")
    group = lax.axis_index("groups")
    core = lax.rem(me, 2)
    side = lax.rem(lax.div(me, 2), 2)
    after, before = lax.rem(me + 1, count), lax.rem(me + count - 1, count)
    reach = count // 4
    quarter = lax.div(me, reach)
    ahead, behind = lax.rem(me + reach, count), lax.rem(me + count - reach, count)
    mine, theirs = core * half, (1 - core) * half

    def bit_at(k):
        return lax.rem(lax.div(me, 1 << k), 2)

    def mate(k):
        return me + (1 - 2 * bit_at(k)) * (1 << k)

    def remote(src, dst, s, r, to):
        return pltpu.make_async_remote_copy(
            src_ref=src, dst_ref=dst, send_sem=s, recv_sem=r,
            device_id=(group, to), device_id_type=MESH,
        )

    cut = 4
    span_cols = [(i * (heads // cut) * LANES, (heads // cut) * LANES) for i in range(cut)]
    span_cols.append((heads * LANES, width - heads * LANES))
    loads = [pltpu.make_async_copy(decay_hbm, decay, load_sem.at[0]), pltpu.make_async_copy(taps_hbm, taps, load_sem.at[1])]
    xloads = [
        pltpu.make_async_copy(xbc_hbm.at[:, pl.ds(at, n)], xbc.at[:, pl.ds(at, n)], load_sem.at[2 + i])
        for i, (at, n) in enumerate(span_cols)
    ]
    late = [pltpu.make_async_copy(lw_hbm, lw, load_sem.at[7]), pltpu.make_async_copy(gain_hbm, gain, load_sem.at[8])]
    for load in loads + xloads + late:
        load.start()
    barrier = pltpu.get_barrier_semaphore()
    for to in [after, before, ahead, behind] + [mate(k) for k in range(seq_bits)]:
        pl.semaphore_signal(barrier, inc=1, device_id=(group, to), device_id_type=MESH)

    tri = (
        lax.broadcasted_iota(jnp.int32, (LANES, LANES), 0)
        <= lax.broadcasted_iota(jnp.int32, (LANES, LANES), 1)
    ).astype(F32).astype(BF16)
    loads[0].wait()
    rest = jnp.concatenate([decay[:, lane(a)] for a in range(tiles)], axis=0)
    parts = []
    for _ in range(3):
        part = rest.astype(BF16)
        rest = rest - part.astype(F32)
        parts.append(part)
    sums = jnp.dot(jnp.concatenate(parts, axis=0), tri, preferred_element_type=F32)
    step = tiles * heads
    sums = sums[2 * step : 3 * step] + sums[step : 2 * step] + sums[0:step]
    ll, base = [], jnp.zeros((heads, LANES), F32)
    for a in range(tiles):
        ll.append(sums[a * heads : (a + 1) * heads] + base)
        base = jnp.broadcast_to(ll[a][:, LANES - 1 :], (heads, LANES))
    total = base
    span[0] = total
    pl.semaphore_wait(barrier, 4 + seq_bits)

    halo_copy = remote(xbc_hbm.at[rows - PACK : rows, :], halo, halo_sem.at[0], halo_sem.at[1], after)

    @pl.when(me < count - 1)
    def _():
        halo_copy.start()

    def span_copy(k):
        return remote(span.at[k], span_rx.at[k], span_send.at[k], span_recv.at[k], mate(k))

    span_copy(0).start()

    mids = [jnp.broadcast_to(x[:, LANES // 2 - 1 : LANES // 2], (heads, LANES)) for x in ll]
    for a in range(tiles):
        tail[:, lane(a)] = jnp.exp(total - ll[a])
        col[:, lane(a)] = jnp.exp(mids[a] - ll[a])

    pad[:, 0:8, :] = jnp.zeros((pad.shape[0], 8, LANES), F32)
    loads[1].wait()

    def activate(ref, lead, first, n, at):
        weights = taps[:, at] * 0.5
        start = first - kern + 1
        total = ref[lead, start : start + n, :] * weights[0:1]
        for k in range(1, kern):
            total = total + ref[lead, start + k : start + k + n, :] * weights[k : k + 1]
        return (total * jnp.tanh(total) + total).astype(BF16)

    unroll = pad.shape[0]
    for i, (at, n) in enumerate(span_cols):
        xloads[i].wait()

        @pl.loop(at // LANES, (at + n) // LANES, step=unroll)
        def _(j):
            for u in range(unroll):
                pad[u, 8 : 8 + rows, :] = xbc[:, lane(j + u)].astype(F32)
                vbuf[:, lane(j + u)] = activate(pad, u, 8, rows, lane(j + u))

    @pl.when(me > 0)
    def _():
        halo_copy.wait_recv()

    @pl.loop(0, width // LANES, step=2)
    def _(j):
        for u in range(2):
            at = lane(j + u)
            edge[j + u, 0:8, :] = jnp.where(me == 0, 0.0, halo[:, at].astype(F32)[PACK - 8 :])
            edge[j + u, 8 : 8 + PACK, :] = xbc[0:PACK, at].astype(F32)
            vbuf[0:PACK, at] = activate(edge, j + u, 8, PACK, at)

    def chunk(o):
        return (1 - side) * 2 + o if o < 2 else side * 2 + o - 2

    def state(o):
        first = [theirs + chunk(o) * per, mine + chunk(o) * per]
        which = [f + u for f in first for u in range(per)]
        for i, h in enumerate(which):
            flipped = jnp.transpose(vbuf[:, lane(h)])
            values_t[h] = flipped * jnp.concatenate([packed(col[pl.ds(h, 1), :])] * (LANES // PACK), axis=0)
            dec[i * LANES : (i + 1) * LANES, :] = flipped * jnp.concatenate(
                [packed(tail[pl.ds(h, 1), :])] * (LANES // PACK), axis=0
            )
        found = jnp.dot(dec[...], vbuf[:, lane(heads)], preferred_element_type=F32)
        for i, h in enumerate(which):
            st = found[i * LANES : (i + 1) * LANES]
            agg[h] = st
            send[0, h] = st.astype(BF16)

    def part(start, c):
        return pl.ds(start + c * per, per)

    def chip_copy(start, c, slot):
        at = part(start, c)
        return remote(send.at[0, at], node.at[0, at], chip_send.at[slot], chip_recv.at[slot], mate(0))

    def to_theirs(o):
        return chip_copy(theirs, chunk(o), chunk(o))

    def to_mine(o):
        return chip_copy(mine, chunk(o), CH + chunk(o))

    def step_copy(k, c):
        at = part(mine, c)
        i = k * CH + c
        return remote(send.at[k, at], node.at[k, at], step_send.at[i], step_recv.at[i], mate(k))

    def last_copy(c, source):
        at = part(mine, c)
        i = last * CH + c
        return remote(source.at[last, at], node.at[last, at], step_send.at[i], step_recv.at[i], ahead)

    def x_forward(k, c):
        at = part(mine, c)
        i = k * CH + c
        return remote(node.at[k, at], node.at[k, at], xf_send.at[i], xf_recv.at[i], mate(1))

    def c_forward(k, c, start=None):
        at = part(mine if start is None else start, c)
        i = k * CH + c
        return remote(node.at[k, at], node.at[k, at], cf_send.at[i], cf_recv.at[i], mate(0))

    def span_step(k):
        span_copy(k).wait_recv()
        other = span_rx[k]
        prefix[k + 1] = prefix[k] + jnp.where(bit_at(k) == 1, other, 0.0)
        span[k + 1] = span[k] + other
        if k + 1 < seq_bits:
            span_copy(k + 1).start()

    def combine(k, c):
        upper = bit_at(k) == 1
        for u in range(per):
            h = mine + c * per + u
            own_span = span[k, pl.ds(h, 1), :]
            other_span = span_rx[k, pl.ds(h, 1), :]
            keep = jnp.exp(jnp.where(upper, own_span, other_span))
            own_factor = jnp.where(upper, 1.0, keep)
            other_factor = jnp.where(upper, keep, 1.0)
            joined = agg[h] * own_factor + node[k, h].astype(F32) * other_factor
            agg[h] = joined
            send[k + 1, h] = joined.astype(BF16)

    def both_ways(k):
        return k < last - 1

    def sends(k, go):
        if both_ways(k):
            go()
        else:
            pl.when(bit_at(k) == 0)(go)

    def join_chip(o):
        c = chunk(o)
        to_theirs(o).wait_recv()
        combine(0, c)
        if o < 2:
            step_copy(1, c).start()
        else:
            @pl.when(side == 0)
            def _():
                step_copy(1, c).start()

    def join_x(o):
        c = chunk(o)
        step_copy(1, c).wait_recv()

        @pl.when(side == 1)
        def _():
            c_forward(1, c).start()

        combine(1, c)
        if last == 2:
            @pl.when(quarter == 1)
            def _():
                last_copy(c, send).start()
        else:
            sends(2, lambda: step_copy(2, c).start())

    def take_x(o):
        c = chunk(o)

        @pl.when(side == 1)
        def _():
            step_copy(1, c).wait_recv()
            c_forward(1, c).start()

    def join(k, o):
        c = chunk(o)

        def arrived():
            step_copy(k, c).wait_recv()

        if both_ways(k):
            arrived()

        @pl.when(bit_at(k) == 1)
        def _():
            if not both_ways(k):
                arrived()
            x_forward(k, c).start()
            c_forward(k, c).start()

        if k + 1 < last:
            combine(k, c)
            sends(k + 1, lambda: step_copy(k + 1, c).start())
        else:
            @pl.when(quarter == 1)
            def _():
                combine(k, c)
                last_copy(c, send).start()

    def take(k, o):
        c = chunk(o)

        @pl.when(bit_at(k) == 1)
        def _():
            x_forward(k, c).wait_recv()
            c_forward(k, c).start()

    def join_last(o):
        c = chunk(o)

        @pl.when(quarter >= 2)
        def _():
            last_copy(c, send).wait_recv()

        @pl.when(quarter == 2)
        def _():
            last_copy(c, node).start()

        @pl.when(quarter >= 2)
        def _():
            x_forward(last, c).start()
            c_forward(last, c).start()

    prefix[0] = jnp.zeros((heads, LANES), F32)
    for o in range(CH):
        state(o)
        to_theirs(o).start()

        @pl.when(core == 0)
        def _():
            to_mine(o).start()

        if o == 0:
            span_step(0)
        else:
            join_chip(o - 1)

    late[0].wait()
    late[1].wait()
    lows = []
    for a in range(tiles):
        low = jnp.exp(ll[a] - mids[a])
        for l in range(tile_bits + 1):
            diag[l, :, lane(a)] = lw[l, :, lane(a)] * low
        for b in range(a):
            level = tile_bits + (a ^ b).bit_length()
            cross[a * (a - 1) // 2 + b] = lw[level, :, lane(a)] * jnp.exp(ll[a] - mids[b])
    join_chip(CH - 1)
    span_step(1)
    out_map_t[...] = jnp.transpose(vbuf[:, lane(heads + 1)])
    s_all = lax.broadcasted_iota(jnp.int32, (LANES, LANES), 0)
    t_all = lax.broadcasted_iota(jnp.int32, (LANES, LANES), 1)
    for b in range(tiles):
        scored = jnp.dot(vbuf[lane(b), lane(heads)], out_map_t[...], preferred_element_type=F32)
        for a in range(b, tiles):
            piece = scored[:, a * LANES : (a + 1) * LANES]
            scores_t[lane(b), lane(a)] = (jnp.where(s_all <= t_all, piece, 0.0) if a == b else piece).astype(BF16)
    flipped_gain = jnp.transpose(jnp.concatenate([gain[...], jnp.zeros((LANES - heads, LANES), F32)], axis=0))
    for h in range(heads):
        gain_col[h] = jnp.broadcast_to(flipped_gain[:, h : h + 1], (LANES, LANES))

    def far_table(k):
        level = local_bits + 1 + k
        for a in range(tiles):
            factor = lw[level, :, lane(a)] * jnp.exp(ll[a] + prefix[k])
            far_row[k, :, lane(a)] = jnp.where(bit_at(k) == 1, factor, 0.0)

    t_in = lax.broadcasted_iota(jnp.int32, (PACK, LANES), 1)
    s_in = lax.broadcasted_iota(jnp.int32, (PACK, LANES), 0)
    fine_bits = PACK.bit_length() - 1
    differ = jnp.bitwise_xor(s_in, jnp.bitwise_and(t_in, PACK - 1))
    t_group = lax.shift_right_logical(t_in, fine_bits)
    groups16 = LANES // PACK
    for u in range(wt.shape[0]):
        for a in range(0, tiles, 2):
            wt[u, lane(a + 1), lane(a)] = jnp.zeros((LANES, LANES), BF16)

    def spread(k, h, u):
        row = packed(far_row[k, pl.ds(h, 1), :])
        for s in range(groups16):
            at = k * LANES + s * PACK
            fw[u, at : at + PACK, :] = out_map_t[s * PACK : (s + 1) * PACK, :] * row

    def weights(h, u):
        for a in range(tiles):
            row = [diag[l, pl.ds(h, 1), lane(a)] for l in range(tile_bits + 1)]
            fine = row[fine_bits]
            for l in range(fine_bits - 1, 0, -1):
                fine = jnp.where(differ < (1 << l), row[l], fine)
            fine = jnp.where(differ == 0, row[0], fine).astype(BF16)
            wide = [packed(r) for r in row[fine_bits + 1 :]]
            for j in range(groups16):
                apart = jnp.bitwise_xor(t_group, j)
                chosen = fine
                for l in range(len(wide)):
                    if any((1 << l) <= (x ^ j) < (2 << l) for x in range(j, groups16)):
                        chosen = jnp.where((apart >= (1 << l)) & (apart < (2 << l)), wide[l], chosen)
                at = a * LANES + j * PACK
                wt[u, at : at + PACK, lane(a)] = chosen * scores_t[at : at + PACK, lane(a)]
            for b in range(a):
                row = packed(cross[a * (a - 1) // 2 + b, pl.ds(h, 1), :])
                for j in range(groups16):
                    at = b * LANES + j * PACK
                    wt[u, at : at + PACK, lane(a)] = row * scores_t[at : at + PACK, lane(a)]

    def held(k, h):
        source = node[k, h]
        return jnp.where(bit_at(k) == 1, source, jnp.zeros_like(source))

    def near(first, n):
        for u in range(n):
            weights(first + u, u)
        for u in range(n):
            h = first + u
            for a in range(0, tiles, 2):
                deep = (a + 2) * LANES
                near_t[h, :, a * LANES : deep] = jnp.dot(
                    values_t[h, :, 0:deep], wt[u, 0:deep, a * LANES : deep], preferred_element_type=F32
                )

    def finish(first, n):
        for u in range(n):
            for k in range(seq_bits):
                spread(k, first + u, u)
        for u in range(n):
            h = first + u
            left = jnp.concatenate([held(k, h) for k in range(seq_bits)], axis=1)
            mixed = near_t[h] + jnp.dot(left, fw[u], preferred_element_type=F32)
            mean = jnp.mean(mixed * mixed, axis=0, keepdims=True)
            scaled = mixed * lax.rsqrt(mean + 1e-05) * jnp.concatenate([gain_col[h]] * tiles, axis=1)
            out[:, lane(h)] = jnp.transpose(scaled.astype(BF16))

    def finish_mine(o):
        finish(mine + chunk(o) * per, per)

    def finish_theirs(o):
        c = chunk(o)

        @pl.when(core == 1)
        def _():
            chip_copy(theirs, c, CH + c).wait_recv()

        for k in range(1, last):
            @pl.when(bit_at(k) == 1)
            def _():
                c_forward(k, c, theirs).wait_recv()

        @pl.when(quarter >= 2)
        def _():
            c_forward(last, c, theirs).wait_recv()

        finish(theirs + c * per, per)

    def take_last(o):
        c = chunk(o)

        @pl.when(quarter >= 2)
        def _():
            x_forward(last, c).wait_recv()
            c_forward(last, c).start()

    batch = wt.shape[0]
    far_table(0)
    far_table(1)
    near(0, batch)
    join_x(2)
    join_x(3)
    near(batch, batch)
    take_x(0)
    take_x(1)
    span_step(2)
    near(2 * batch, batch)
    for k in range(2, last):
        if k > 2:
            span_step(k)
        far_table(k)
        join(k, 2)
        join(k, 3)
        if k == 2:
            near(3 * batch, batch)
        take(k, 0)
        take(k, 1)
    if last > 2:
        span_step(last)
    far_table(last)
    join_last(2)
    join_last(3)
    finish_mine(2)
    finish_mine(3)
    take_last(0)
    take_last(1)
    finish_theirs(2)
    finish_mine(0)
    finish_theirs(3)
    finish_mine(1)
    finish_theirs(0)
    finish_theirs(1)

    @pl.when(me < count - 1)
    def _():
        halo_copy.wait_send()

    for k in range(seq_bits):
        span_copy(k).wait_send()
    for o in range(CH):
        c = chunk(o)
        to_theirs(o).wait_send()

        @pl.when(core == 0)
        def _():
            to_mine(o).wait_send()

        if o < 2:
            step_copy(1, c).wait_send()
        else:
            @pl.when(side == 0)
            def _():
                step_copy(1, c).wait_send()

        @pl.when(side == 1)
        def _():
            c_forward(1, c).wait_send()

        for k in range(2, last):
            if o >= 2:
                sends(k, lambda: step_copy(k, c).wait_send())

            @pl.when(bit_at(k) == 1)
            def _():
                if o >= 2:
                    x_forward(k, c).wait_send()
                c_forward(k, c).wait_send()

        if o >= 2:
            @pl.when(quarter == 1)
            def _():
                last_copy(c, send).wait_send()

            @pl.when(quarter == 2)
            def _():
                last_copy(c, node).wait_send()

        @pl.when(quarter >= 2)
        def _():
            if o >= 2:
                x_forward(last, c).wait_send()
            c_forward(last, c).wait_send()


def on_device(xbc, conv_weight, log_decay, level_weights, gain):
    rows, width = xbc.shape
    heads = log_decay.shape[0]
    inner = gain.shape[0]
    dim = inner // heads
    tiles = rows // LANES
    levels = level_weights.shape[1]
    seq_bits = lax.axis_size("seq").bit_length() - 1
    dma = pltpu.SemaphoreType.DMA
    hbm = pl.BlockSpec(memory_space=pltpu.HBM)
    square = (heads, dim, LANES)
    return pl.pallas_call(
        functools.partial(kernel, seq_bits),
        out_shape=pltpu.VMEM((rows, inner), BF16),
        in_specs=[hbm] * 5,
        out_specs=pl.BlockSpec(memory_space=pltpu.VMEM),
        scratch_shapes=[
            pltpu.VMEM((rows, width), BF16),
            pltpu.VMEM(conv_weight.shape, F32),
            pltpu.VMEM((heads, rows), F32),
            pltpu.VMEM((levels, heads, rows), F32),
            pltpu.VMEM((heads, dim), F32),
            dma((9,)),
            pltpu.VMEM((2, rows + 8, LANES), F32),
            pltpu.VMEM((width // LANES, PACK + 8, LANES), F32),
            pltpu.VMEM((PACK, width), BF16),
            pltpu.VMEM((rows, width), BF16),
            pltpu.VMEM((LANES, rows), BF16),
            pltpu.VMEM((heads, dim, rows), BF16),
            pltpu.VMEM((heads // 4 * dim, rows), BF16),
            pltpu.VMEM((heads, rows), F32),
            pltpu.VMEM((heads, rows), F32),
            pltpu.VMEM((LANES.bit_length(), heads, rows), F32),
            pltpu.VMEM((tiles * (tiles - 1) // 2, heads, LANES), F32),
            pltpu.VMEM((seq_bits, heads, rows), F32),
            pltpu.VMEM((rows, rows), BF16),
            pltpu.VMEM((heads // 4, rows, rows), BF16),
            pltpu.VMEM((heads // 8, seq_bits * LANES, rows), BF16),
            pltpu.VMEM((heads, dim, rows), F32),
            pltpu.VMEM(square, F32),
            pltpu.VMEM(square, F32),
            pltpu.VMEM((seq_bits,) + square, BF16),
            pltpu.VMEM((seq_bits,) + square, BF16),
            pltpu.VMEM((seq_bits + 1, heads, LANES), F32),
            pltpu.VMEM((seq_bits, heads, LANES), F32),
            pltpu.VMEM((seq_bits + 1, heads, LANES), F32),
            dma((2,)),
            dma((seq_bits,)),
            dma((seq_bits,)),
            dma((8,)),
            dma((8,)),
            dma((seq_bits * 4,)),
            dma((seq_bits * 4,)),
            dma((seq_bits * 4,)),
            dma((seq_bits * 4,)),
            dma((seq_bits * 4,)),
            dma((seq_bits * 4,)),
        ],
        compiler_params=pltpu.CompilerParams(
            collective_id=0, has_side_effects=True, vmem_limit_bytes=61 * 1024 * 1024
        ),
        name="mixer",
    )(xbc, conv_weight, log_decay, level_weights.transpose(1, 0, 2), gain.reshape(heads, dim))


def solution(mesh):
    in_specs = (
        P(("groups", "seq"), None),
        P(),
        P(None, ("groups", "seq")),
        P(None, None, ("groups", "seq")),
        P(),
    )
    out_specs = P(("groups", "seq"), None)
    return jax.shard_map(
        on_device, mesh=mesh, in_specs=in_specs, out_specs=out_specs, check_vma=False
    )
```

```python
import functools
import jax
import jax.numpy as jnp
from jax import lax
from jax.experimental import pallas as pl
from jax.experimental.pallas import tpu as pltpu
from jax.sharding import PartitionSpec as P

LANES = 128
PACK = 16
MESH = pl.DeviceIdType.MESH
F32, BF16 = jnp.float32, jnp.bfloat16


def lane(i, width=LANES):
    if isinstance(i, int):
        return pl.ds(i * width, width)
    return pl.ds(pl.multiple_of(i * width, LANES), width)


def packed(row, times=1):
    return jnp.broadcast_to(row, (PACK * times, row.shape[1])).astype(BF16)


def kernel(
    seq_bits, xbc_hbm, taps_hbm, decay_hbm, lw_hbm, gain_hbm, out,
    xbc, taps, decay, lw, gain, load_sem, pad, edge, halo, vbuf, out_map_t, values_t, dec,
    tail, col, diag, cross, far_row, scores_t, wt, fw, near_t, gain_col,
    agg, send, node, span, span_rx, prefix, factor,
    halo_sem, span_send, span_recv, chip_send, chip_recv, step_send, step_recv, last_send, last_recv, xf_send, xf_recv, cf_send, cf_recv,
):
    rows, width = xbc.shape
    heads = decay.shape[0]
    kern = taps.shape[0]
    half = heads // 2
    own = half // 2
    tiles = rows // LANES
    tile_bits = LANES.bit_length() - 1
    local_bits = rows.bit_length() - 1
    count = 1 << seq_bits
    last = seq_bits - 1
    me = lax.axis_index("seq")
    group = lax.axis_index("groups")
    core = lax.rem(me, 2)
    side = lax.rem(lax.div(me, 2), 2)
    after, before = lax.rem(me + 1, count), lax.rem(me + count - 1, count)
    reach = count // 4
    quarter = lax.div(me, reach)
    ahead = lax.rem(me + reach, count)
    mine, theirs = core * half, (1 - core) * half

    def bit_at(k):
        return lax.rem(lax.div(me, 1 << k), 2)

    def mate(k):
        return me + (1 - 2 * bit_at(k)) * (1 << k)

    def remote(src, dst, s, r, to):
        return pltpu.make_async_remote_copy(
            src_ref=src, dst_ref=dst, send_sem=s, recv_sem=r,
            device_id=(group, to), device_id_type=MESH,
        )

    cut = 4
    some = heads // cut
    loads = [pltpu.make_async_copy(decay_hbm, decay, load_sem.at[0]), pltpu.make_async_copy(taps_hbm, taps, load_sem.at[1])]

    def xload(i):
        at = pl.ds(heads * LANES, width - heads * LANES) if i is None else lane(i, some * LANES)
        return pltpu.make_async_copy(xbc_hbm.at[:, at], xbc.at[:, at], load_sem.at[2 + cut if i is None else 2 + i])

    xloads = [xload(None)] + [xload(i) for i in range(cut)]
    late = [pltpu.make_async_copy(lw_hbm, lw, load_sem.at[3 + cut]), pltpu.make_async_copy(gain_hbm, gain, load_sem.at[4 + cut])]
    for load in loads + xloads + late:
        load.start()
    barrier = pltpu.get_barrier_semaphore()
    partners = [
        (me < count - 1, after), (me > 0, before),
        (quarter == 1, ahead), (quarter == 1, lax.rem(me + 2 * reach, count)),
        (quarter >= 2, lax.rem(me + count - (quarter - 1) * reach, count)),
    ] + [(None, mate(k)) for k in range(last)]
    expected = 0
    for there, to in partners:
        def greet():
            pl.semaphore_signal(barrier, inc=1, device_id=(group, to), device_id_type=MESH)

        if there is None:
            greet()
            expected = expected + 1
        else:
            pl.when(there)(greet)
            expected = expected + there.astype(jnp.int32)
    tri = (
        lax.broadcasted_iota(jnp.int32, (LANES, LANES), 0)
        <= lax.broadcasted_iota(jnp.int32, (LANES, LANES), 1)
    ).astype(F32).astype(BF16)
    loads[0].wait()
    rest = jnp.concatenate([decay[:, lane(a)] for a in range(tiles)], axis=0)
    parts = []
    for _ in range(3):
        part = rest.astype(BF16)
        rest = rest - part.astype(F32)
        parts.append(part)
    sums = jnp.dot(jnp.concatenate(parts, axis=0), tri, preferred_element_type=F32)
    step = tiles * heads
    sums = sums[2 * step : 3 * step] + sums[step : 2 * step] + sums[0:step]
    ll, base = [], jnp.zeros((heads, LANES), F32)
    for a in range(tiles):
        ll.append(sums[a * heads : (a + 1) * heads] + base)
        base = jnp.broadcast_to(ll[a][:, LANES - 1 :], (heads, LANES))
    total = base
    span[0] = total

    pad[:, 0:8, :] = jnp.zeros((pad.shape[0], 8, LANES), F32)
    loads[1].wait()

    def activate(ref, lead, first, n, at):
        weights = taps[:, at] * 0.5
        start = first - kern + 1
        total = ref[lead, start : start + n, :] * weights[0:1]
        for k in range(1, kern):
            total = total + ref[lead, start + k : start + k + n, :] * weights[k : k + 1]
        return (total * jnp.tanh(total) + total).astype(BF16)

    def convolve(j, u):
        pad[u, 8 : 8 + rows, :] = xbc[:, lane(j)].astype(F32)
        vbuf[:, lane(j)] = activate(pad, u, 8, rows, lane(j))

    xloads[0].wait()
    for u in range(width // LANES - heads):
        convolve(heads + u, u)

    def convolve_group(i):
        xload(i).wait()
        for u in range(some):
            convolve(i * some + u, u)

    pl.semaphore_wait(barrier, expected)
    halo_copy = remote(xbc_hbm.at[rows - PACK : rows, :], halo, halo_sem.at[0], halo_sem.at[1], after)

    @pl.when(me < count - 1)
    def _():
        halo_copy.start()


    def span_copy(k):
        return remote(span.at[k], span_rx.at[k], span_send.at[k], span_recv.at[k], mate(k))

    span_copy(0).start()

    mids = [jnp.broadcast_to(x[:, LANES // 2 - 1 : LANES // 2], (heads, LANES)) for x in ll]
    for a in range(tiles):
        tail[:, lane(a)] = jnp.exp(total - ll[a])
        col[:, lane(a)] = jnp.exp(mids[a] - ll[a])

    def span_step(k):
        span_copy(k).wait_recv()
        other = span_rx[k]
        upper = bit_at(k) == 1
        prefix[k + 1] = prefix[k] + jnp.where(upper, other, 0.0)
        keep = jnp.exp(jnp.where(upper, span[k], other))
        factor[0, k] = jnp.where(upper, 1.0, keep)
        factor[1, k] = jnp.where(upper, keep, 1.0)
        span[k + 1] = span[k] + other
        if k + 1 < last:
            span_copy(k + 1).start()

    prefix[0] = jnp.zeros((heads, LANES), F32)
    convolve_group(0)

    def spread_rows(ref, h, first, last_tile):
        row = packed(ref[pl.ds(h, 1), :][:, first * LANES : last_tile * LANES])
        return jnp.concatenate([row] * (LANES // PACK), axis=0)

    def turn(h, i, first, last_tile):
        at = slice(first * LANES, last_tile * LANES)
        flipped = jnp.transpose(vbuf[at, lane(h)])
        values_t[h, :, at] = flipped * spread_rows(col, h, first, last_tile)
        dec[lane(i), at] = flipped * spread_rows(tail, h, first, last_tile)

    def sum_main(g):
        found = jnp.dot(dec[0 : some * LANES, LANES:rows], vbuf[LANES:rows, lane(heads)], preferred_element_type=F32)
        for u in range(some):
            agg[g * some + u] = found[u * LANES : (u + 1) * LANES]

    def overlap(i):
        for u in range(some):
            turn((i - 1) * some + u, u, 1, tiles)
        convolve_group(i)
        sum_main(i - 1)

    overlap(1)
    span_step(0)
    pl.loop(2, cut)(overlap)
    for u in range(some):
        turn((cut - 1) * some + u, u, 1, tiles)
    sum_main(cut - 1)

    span_step(1)

    @pl.when(me > 0)
    def _():
        halo_copy.wait_recv()

    @pl.loop(0, width // LANES, step=6)
    def _(j):
        for u in range(6):
            at = lane(j + u)
            edge[j + u, 0:8, :] = jnp.where(me == 0, 0.0, halo[:, at].astype(F32)[PACK - 8 :])
            edge[j + u, 8 : 8 + PACK, :] = xbc[0:PACK, at].astype(F32)
            vbuf[0:PACK, at] = activate(edge, j + u, 8, PACK, at)

    def chunk(o):
        return (1 - side) * own + o if o < own else side * own + o - own

    def state(some):
        which = [start + chunk(o) for o in some for start in (theirs, mine)]
        base = 2 * some[0]
        for i, h in enumerate(which):
            turn(h, base + i, 0, 1)
        found = jnp.dot(
            dec[base * LANES : (base + len(which)) * LANES, 0:LANES], vbuf[0:LANES, lane(heads)], preferred_element_type=F32
        )
        for i, h in enumerate(which):
            st = agg[h] + found[i * LANES : (i + 1) * LANES]
            agg[h] = st
            send[0, h] = st.astype(BF16)

    def part(start, o, n):
        if n == half:
            return pl.ds(start, half)
        return pl.ds(start + chunk(o), n)

    def side_of(o):
        return 1 - side if o < own else side

    def to_theirs(o, n=1):
        at = part(theirs, o, n)
        return remote(send.at[0, at], node.at[0, at], chip_send.at[0], chip_recv.at[side_of(o)], mate(0))

    def from_mate(o):
        at = part(mine, o, own)
        return remote(send.at[0, at], node.at[0, at], chip_send.at[0], chip_recv.at[side_of(o)], mate(0))

    def to_mine(o, n=1, start=mine):
        at = part(start, o, n)
        return remote(send.at[0, at], node.at[0, at], chip_send.at[1], chip_recv.at[2 + side_of(o)], mate(0))

    def step_copy(k, o, n=1):
        at = part(mine, o, n)
        if k == 1:
            s, r = step_send.at[o // own], step_recv.at[0 if n > 1 else chunk(o)]
        else:
            s, r = step_send.at[k], step_recv.at[half + (k - 2) * own + o - own]
        return remote(send.at[k, at], node.at[k, at], s, r, mate(k))

    def last_copy(o, hops=1, n=1):
        at = part(mine, o, n)
        to = lax.rem(me + hops * reach, count)
        return remote(send.at[last, at], node.at[last, at], last_send.at[hops - 1], last_recv.at[o - own], to)

    def last_start(o):
        for hops in (2, 1):
            last_copy(o, hops).start()

    def x_forward(k, o, n=1):
        at = part(mine, o, n)
        return remote(node.at[k, at], node.at[k, at], xf_send.at[k - 2], xf_recv.at[(k - 2) * own + o % own], mate(1))

    def c_forward(k, o, n=1, start=mine):
        at = part(start, o, n)
        return remote(node.at[k, at], node.at[k, at], cf_send.at[k - 1], cf_recv.at[2 * (k - 1) + side_of(o)], mate(0))

    def combine(k, c):
        h = mine + c
        joined = agg[h] * factor[0, k, pl.ds(h, 1), :] + node[k, h].astype(F32) * factor[1, k, pl.ds(h, 1), :]
        agg[h] = joined
        send[k + 1, h] = joined.astype(BF16)

    def both_ways(k):
        return k < last - 1

    def sends(k, go):
        if both_ways(k):
            go()
        else:
            pl.when(bit_at(k) == 0)(go)

    def join_chip(which):
        from_mate(which[0]).wait_recv()
        for o in which:
            combine(0, chunk(o))
        if which[0] < own:
            for o in which:
                step_copy(1, o).start()
        else:
            @pl.when(side == 0)
            def _():
                for o in which:
                    step_copy(1, o).start()

    def join_x(o):
        step_copy(1, o).wait_recv()

        @pl.when(side == 1)
        def _():
            c_forward(1, o).start()

        combine(1, chunk(o))
        if last == 2:
            @pl.when(quarter == 1)
            def _():
                last_start(o)
        else:
            sends(2, lambda: step_copy(2, o).start())

    def take_x(o):
        @pl.when(side == 1)
        def _():
            step_copy(1, o).wait_recv()
            c_forward(1, o).start()

    def join(k, o):
        if both_ways(k):
            step_copy(k, o).wait_recv()

        @pl.when(bit_at(k) == 1)
        def _():
            if not both_ways(k):
                step_copy(k, o).wait_recv()
            x_forward(k, o).start()
            c_forward(k, o).start()

        if k + 1 < last:
            combine(k, chunk(o))
            sends(k + 1, lambda: step_copy(k + 1, o).start())
        else:
            @pl.when(quarter == 1)
            def _():
                combine(k, chunk(o))
                last_start(o)

    def take(k, o):
        @pl.when(bit_at(k) == 1)
        def _():
            x_forward(k, o).wait_recv()
            c_forward(k, o).start()

    def join_last(o):
        @pl.when(quarter >= 2)
        def _():
            last_copy(o).wait_recv()
            x_forward(last, o).start()
            c_forward(last, o).start()

    for o in range(0, half, 2):
        state((o, o + 1))
    for o in range(half):
        to_theirs(o).start()

    @pl.when(core == 0)
    def _():
        for o in range(half):
            to_mine(o).start()

    join_chip(range(own))
    join_chip(range(own, half))

    late[0].wait()
    late[1].wait()
    lows = []
    for a in range(tiles):
        low = jnp.exp(ll[a] - mids[a])
        for l in range(tile_bits + 1):
            diag[l, :, lane(a)] = lw[l, :, lane(a)] * low
        for b in range(a):
            level = tile_bits + (a ^ b).bit_length()
            cross[a * (a - 1) // 2 + b] = lw[level, :, lane(a)] * jnp.exp(ll[a] - mids[b])
    out_map_t[...] = jnp.transpose(vbuf[:, lane(heads + 1)])
    s_all = lax.broadcasted_iota(jnp.int32, (LANES, LANES), 0)
    t_all = lax.broadcasted_iota(jnp.int32, (LANES, LANES), 1)
    for b in range(tiles):
        scored = jnp.dot(vbuf[lane(b), lane(heads)], out_map_t[...], preferred_element_type=F32)
        for a in range(b, tiles):
            piece = scored[:, a * LANES : (a + 1) * LANES]
            scores_t[lane(b), lane(a)] = (jnp.where(s_all <= t_all, piece, 0.0) if a == b else piece).astype(BF16)
    flipped_gain = jnp.transpose(jnp.concatenate([gain[...], jnp.zeros((LANES - heads, LANES), F32)], axis=0))
    for h in range(heads):
        gain_col[h] = jnp.broadcast_to(flipped_gain[:, h : h + 1], (LANES, LANES))

    def far_table(k):
        level = local_bits + 1 + k
        for a in range(tiles):
            factor = lw[level, :, lane(a)] * jnp.exp(ll[a] + prefix[k])
            far_row[k, :, lane(a)] = jnp.where(bit_at(k) == 1, factor, 0.0)

    t_in = lax.broadcasted_iota(jnp.int32, (PACK, LANES), 1)
    s_in = lax.broadcasted_iota(jnp.int32, (PACK, LANES), 0)
    fine_bits = PACK.bit_length() - 1
    differ = jnp.bitwise_xor(s_in, jnp.bitwise_and(t_in, PACK - 1))
    t_group = lax.shift_right_logical(t_in, fine_bits)
    groups16 = LANES // PACK
    for u in range(wt.shape[0]):
        for a in range(0, tiles, 2):
            wt[u, lane(a + 1), lane(a)] = jnp.zeros((LANES, LANES), BF16)

    def spread(k, h, u):
        row = packed(far_row[k, pl.ds(h, 1), :])
        for s in range(groups16):
            at = k * LANES + s * PACK
            fw[u, at : at + PACK, :] = out_map_t[s * PACK : (s + 1) * PACK, :] * row

    def weights(h, u):
        for a in range(tiles):
            row = [diag[l, pl.ds(h, 1), lane(a)] for l in range(tile_bits + 1)]
            fine = row[fine_bits]
            for l in range(fine_bits - 1, 0, -1):
                fine = jnp.where(differ < (1 << l), row[l], fine)
            fine = jnp.where(differ == 0, row[0], fine).astype(BF16)
            wide = [packed(r) for r in row[fine_bits + 1 :]]
            for j in range(groups16):
                apart = jnp.bitwise_xor(t_group, j)
                chosen = fine
                for l in range(len(wide)):
                    if any((1 << l) <= (x ^ j) < (2 << l) for x in range(j, groups16)):
                        chosen = jnp.where((apart >= (1 << l)) & (apart < (2 << l)), wide[l], chosen)
                at = a * LANES + j * PACK
                wt[u, at : at + PACK, lane(a)] = chosen * scores_t[at : at + PACK, lane(a)]
            for b in range(a):
                row = packed(cross[a * (a - 1) // 2 + b, pl.ds(h, 1), :])
                for j in range(groups16):
                    at = b * LANES + j * PACK
                    wt[u, at : at + PACK, lane(a)] = row * scores_t[at : at + PACK, lane(a)]

    def held(k, h):
        source = node[k, h]
        return jnp.where(bit_at(k) == 1, source, jnp.zeros_like(source))

    def near(first, n):
        for u in range(n):
            weights(first + u, u)
        for u in range(n):
            h = first + u
            for a in range(0, tiles, 2):
                deep = (a + 2) * LANES
                near_t[h, :, a * LANES : deep] = jnp.dot(
                    values_t[h, :, 0:deep], wt[u, 0:deep, a * LANES : deep], preferred_element_type=F32
                )

    def finish(first, n):
        for u in range(n):
            for k in range(seq_bits):
                spread(k, first + u, u)
        for u in range(n):
            h = first + u
            left = jnp.concatenate([held(k, h) for k in range(seq_bits)], axis=1)
            mixed = near_t[h] + jnp.dot(left, fw[u], preferred_element_type=F32)
            mean = jnp.mean(mixed * mixed, axis=0, keepdims=True)
            scaled = mixed * lax.rsqrt(mean + 1e-05) * jnp.concatenate([gain_col[h]] * tiles, axis=1)
            out[:, lane(h)] = jnp.transpose(scaled.astype(BF16))

    def finish_mine(o):
        finish(mine + chunk(o), own)

    def finish_theirs(o):
        @pl.when(core == 1)
        def _():
            to_mine(o, own, theirs).wait_recv()

        for k in range(1, last):
            @pl.when(bit_at(k) == 1)
            def _():
                c_forward(k, o, own, theirs).wait_recv()

        @pl.when(quarter >= 2)
        def _():
            c_forward(last, o, own, theirs).wait_recv()

        finish(theirs + chunk(o), own)

    def take_last(o):
        @pl.when(quarter >= 2)
        def _():
            x_forward(last, o).wait_recv()
            c_forward(last, o).start()

    batch = wt.shape[0]
    far_table(0)
    far_table(1)
    other, kept = range(own), range(own, half)
    near(0, batch)
    for o in kept[: own // 2]:
        join_x(o)
    near(batch, batch)
    for o in kept[own // 2 :]:
        join_x(o)
    near(2 * batch, batch)
    if last > 2:
        span_step(2)
    for k in range(2, last):
        if k > 2:
            span_step(k)
        far_table(k)
        for o in kept:
            join(k, o)
        if k == 2:
            for o in other:
                take_x(o)
            near(3 * batch, batch)
        for o in other:
            take(k, o)
    far_table(last)
    for o in kept:
        join_last(o)
    finish_mine(own)
    finish_theirs(own)
    for o in other:
        take_last(o)
    finish_mine(0)
    finish_theirs(0)

    @pl.when(me < count - 1)
    def _():
        halo_copy.wait_send()

    for k in range(last):
        span_copy(k).wait_send()
    to_theirs(0, half).wait_send()
    step_copy(1, 0, own).wait_send()

    @pl.when(core == 0)
    def _():
        to_mine(0, half).wait_send()

    @pl.when(side == 0)
    def _():
        step_copy(1, own, own).wait_send()

    @pl.when(side == 1)
    def _():
        c_forward(1, 0, half).wait_send()

    for k in range(2, last):
        sends(k, lambda: step_copy(k, own, own).wait_send())

        @pl.when(bit_at(k) == 1)
        def _():
            x_forward(k, own, own).wait_send()
            c_forward(k, 0, half).wait_send()

    @pl.when(quarter == 1)
    def _():
        for hops in (1, 2):
            last_copy(own, hops, own).wait_send()

    @pl.when(quarter >= 2)
    def _():
        x_forward(last, own, own).wait_send()
        c_forward(last, 0, half).wait_send()


def on_device(xbc, conv_weight, log_decay, level_weights, gain):
    rows, width = xbc.shape
    heads = log_decay.shape[0]
    inner = gain.shape[0]
    dim = inner // heads
    tiles = rows // LANES
    levels = level_weights.shape[1]
    seq_bits = lax.axis_size("seq").bit_length() - 1
    last = seq_bits - 1
    dma = pltpu.SemaphoreType.DMA
    hbm = pl.BlockSpec(memory_space=pltpu.HBM)
    square = (heads, dim, LANES)
    return pl.pallas_call(
        functools.partial(kernel, seq_bits),
        out_shape=pltpu.VMEM((rows, inner), BF16),
        in_specs=[hbm] * 5,
        out_specs=pl.BlockSpec(memory_space=pltpu.VMEM),
        scratch_shapes=[
            pltpu.VMEM((rows, width), BF16),
            pltpu.VMEM(conv_weight.shape, F32),
            pltpu.VMEM((heads, rows), F32),
            pltpu.VMEM((levels, heads, rows), F32),
            pltpu.VMEM((heads, dim), F32),
            dma((9,)),
            pltpu.VMEM((heads // 4, rows + 8, LANES), F32),
            pltpu.VMEM((width // LANES, PACK + 8, LANES), F32),
            pltpu.VMEM((PACK, width), BF16),
            pltpu.VMEM((rows, width), BF16),
            pltpu.VMEM((LANES, rows), BF16),
            pltpu.VMEM((heads, dim, rows), BF16),
            pltpu.VMEM((heads * dim, rows), BF16),
            pltpu.VMEM((heads, rows), F32),
            pltpu.VMEM((heads, rows), F32),
            pltpu.VMEM((LANES.bit_length(), heads, rows), F32),
            pltpu.VMEM((tiles * (tiles - 1) // 2, heads, LANES), F32),
            pltpu.VMEM((seq_bits, heads, rows), F32),
            pltpu.VMEM((rows, rows), BF16),
            pltpu.VMEM((heads // 4, rows, rows), BF16),
            pltpu.VMEM((heads // 4, seq_bits * LANES, rows), BF16),
            pltpu.VMEM((heads, dim, rows), F32),
            pltpu.VMEM(square, F32),
            pltpu.VMEM(square, F32),
            pltpu.VMEM((seq_bits,) + square, BF16),
            pltpu.VMEM((seq_bits,) + square, BF16),
            pltpu.VMEM((seq_bits + 1, heads, LANES), F32),
            pltpu.VMEM((seq_bits, heads, LANES), F32),
            pltpu.VMEM((seq_bits + 1, heads, LANES), F32),
            pltpu.VMEM((2, seq_bits, heads, LANES), F32),
            dma((2,)),
            dma((last,)),
            dma((last,)),
            dma((2,)),
            dma((4,)),
            dma((last,)),
            dma((heads // 2 + (last - 2) * heads // 4,)),
            dma((2,)),
            dma((heads // 4,)),
            dma((last - 1,)),
            dma(((last - 1) * heads // 4,)),
            dma((last,)),
            dma((2 * last,)),
        ],
        compiler_params=pltpu.CompilerParams(
            collective_id=0, has_side_effects=True, vmem_limit_bytes=61 * 1024 * 1024
        ),
        name="mixer",
    )(xbc, conv_weight, log_decay, level_weights.transpose(1, 0, 2), gain.reshape(heads, dim))


def solution(mesh):
    in_specs = (
        P(("groups", "seq"), None),
        P(),
        P(None, ("groups", "seq")),
        P(None, None, ("groups", "seq")),
        P(),
    )
    out_specs = P(("groups", "seq"), None)
    return jax.shard_map(
        on_device, mesh=mesh, in_specs=in_specs, out_specs=out_specs, check_vma=False
    )
```

```python
import functools
import jax
import jax.numpy as jnp
from jax import lax
from jax.experimental import pallas as pl
from jax.experimental.pallas import tpu as pltpu
from jax.sharding import PartitionSpec as P

LANES = 128
PACK = 16
MESH = pl.DeviceIdType.MESH
F32, BF16 = jnp.float32, jnp.bfloat16


def lane(i, width=LANES):
    if isinstance(i, int):
        return pl.ds(i * width, width)
    return pl.ds(pl.multiple_of(i * width, LANES), width)


def packed(row, times=1):
    return jnp.broadcast_to(row, (PACK * times, row.shape[1])).astype(BF16)


def kernel(
    seq_bits, xbc_hbm, taps_hbm, decay_hbm, lw_hbm, gain_hbm, out,
    xbc, taps, decay, lw, gain, load_sem, pad, edge, halo, v_first, v_rest, maps, out_map_t, values_t, dec,
    tail, col, diag, cross, far_row, scores_t, wt, fw, near_t, gain_col,
    agg, send, node, span, span_rx, prefix, factor,
    halo_sem, span_send, span_recv, chip_send, chip_recv, step_send, step_recv, last_send, last_recv, xf_send, xf_recv, cf_send, cf_recv,
):
    rows, width = xbc.shape
    heads = decay.shape[0]
    kern = taps.shape[0]
    half = heads // 2
    own = half // 2
    tiles = rows // LANES
    tile_bits = LANES.bit_length() - 1
    local_bits = rows.bit_length() - 1
    count = 1 << seq_bits
    last = seq_bits - 1
    me = lax.axis_index("seq")
    group = lax.axis_index("groups")
    core = lax.rem(me, 2)
    side = lax.rem(lax.div(me, 2), 2)
    after, before = lax.rem(me + 1, count), lax.rem(me + count - 1, count)
    reach = count // 4
    quarter = lax.div(me, reach)
    ahead = lax.rem(me + reach, count)
    mine, theirs = core * half, (1 - core) * half

    def bit_at(k):
        return lax.rem(lax.div(me, 1 << k), 2)

    def mate(k):
        return me + (1 - 2 * bit_at(k)) * (1 << k)

    def remote(src, dst, s, r, to):
        return pltpu.make_async_remote_copy(
            src_ref=src, dst_ref=dst, send_sem=s, recv_sem=r,
            device_id=(group, to), device_id_type=MESH,
        )

    cut = 4
    some = heads // cut
    loads = [pltpu.make_async_copy(decay_hbm, decay, load_sem.at[0]), pltpu.make_async_copy(taps_hbm, taps, load_sem.at[1])]

    def xload(i):
        at = pl.ds(heads * LANES, width - heads * LANES) if i is None else lane(i, some * LANES)
        return pltpu.make_async_copy(xbc_hbm.at[:, at], xbc.at[:, at], load_sem.at[2 + cut if i is None else 2 + i])

    xloads = [xload(None)] + [xload(i) for i in range(cut)]
    late = [pltpu.make_async_copy(lw_hbm, lw, load_sem.at[3 + cut]), pltpu.make_async_copy(gain_hbm, gain, load_sem.at[4 + cut])]
    for load in loads + xloads + late:
        load.start()
    barrier = pltpu.get_barrier_semaphore()
    partners = [
        (me < count - 1, after), (me > 0, before),
        (quarter == 1, ahead), (quarter == 1, lax.rem(me + 2 * reach, count)),
        (quarter >= 2, lax.rem(me + count - (quarter - 1) * reach, count)),
    ] + [(None, mate(k)) for k in range(last)]
    expected = 0
    for there, to in partners:
        def greet():
            pl.semaphore_signal(barrier, inc=1, device_id=(group, to), device_id_type=MESH)

        if there is None:
            greet()
            expected = expected + 1
        else:
            pl.when(there)(greet)
            expected = expected + there.astype(jnp.int32)
    tri = (
        lax.broadcasted_iota(jnp.int32, (LANES, LANES), 0)
        <= lax.broadcasted_iota(jnp.int32, (LANES, LANES), 1)
    ).astype(F32).astype(BF16)
    loads[0].wait()
    rest = jnp.concatenate([decay[:, lane(a)] for a in range(tiles)], axis=0)
    parts = []
    for _ in range(3):
        part = rest.astype(BF16)
        rest = rest - part.astype(F32)
        parts.append(part)
    sums = jnp.dot(jnp.concatenate(parts, axis=0), tri, preferred_element_type=F32)
    step = tiles * heads
    sums = sums[2 * step : 3 * step] + sums[step : 2 * step] + sums[0:step]
    ll, base = [], jnp.zeros((heads, LANES), F32)
    for a in range(tiles):
        ll.append(sums[a * heads : (a + 1) * heads] + base)
        base = jnp.broadcast_to(ll[a][:, LANES - 1 :], (heads, LANES))
    total = base
    span[0] = total

    pad[:, 0:8, :] = jnp.zeros((pad.shape[0], 8, LANES), F32)
    loads[1].wait()

    def activate(ref, lead, first, n, at):
        weights = taps[:, at] * 0.5
        start = first - kern + 1
        total = ref[lead, start : start + n, :] * weights[0:1]
        for k in range(1, kern):
            total = total + ref[lead, start + k : start + k + n, :] * weights[k : k + 1]
        return (total * jnp.tanh(total) + total).astype(BF16)

    def convolve(j, u):
        pad[u, 8 : 8 + rows, :] = xbc[:, lane(j)].astype(F32)
        return activate(pad, u, 8, rows, lane(j))

    xloads[0].wait()
    for u in range(width // LANES - heads):
        maps[:, lane(u)] = convolve(heads + u, u)

    def convolve_group(i):
        for u in range(some):
            done = convolve(i * some + u, i % 2 * some + u)
            v_first[:, lane(i * some + u)] = done[0:LANES]
            v_rest[i, :, lane(u)] = done[LANES:rows]

    pl.semaphore_wait(barrier, expected)
    halo_copy = remote(xbc_hbm.at[rows - PACK : rows, :], halo, halo_sem.at[0], halo_sem.at[1], after)

    @pl.when(me < count - 1)
    def _():
        halo_copy.start()


    def span_copy(k):
        return remote(span.at[k], span_rx.at[k], span_send.at[k], span_recv.at[k], mate(k))

    span_copy(0).start()

    mids = [jnp.broadcast_to(x[:, LANES // 2 - 1 : LANES // 2], (heads, LANES)) for x in ll]
    for a in range(tiles):
        tail[:, lane(a)] = jnp.exp(total - ll[a])
        col[:, lane(a)] = jnp.exp(mids[a] - ll[a])

    def span_step(k):
        span_copy(k).wait_recv()
        other = span_rx[k]
        upper = bit_at(k) == 1
        prefix[k + 1] = prefix[k] + jnp.where(upper, other, 0.0)
        keep = jnp.exp(jnp.where(upper, span[k], other))
        factor[0, k] = jnp.where(upper, 1.0, keep)
        factor[1, k] = jnp.where(upper, keep, 1.0)
        span[k + 1] = span[k] + other
        if k + 1 < last:
            span_copy(k + 1).start()

    prefix[0] = jnp.zeros((heads, LANES), F32)
    xload(0).wait()
    convolve_group(0)

    def spread_rows(ref, h, first, last_tile):
        row = packed(ref[pl.ds(h, 1), :][:, first * LANES : last_tile * LANES])
        return jnp.concatenate([row] * (LANES // PACK), axis=0)

    def turn(h, i, first, last_tile):
        at = slice(first * LANES, last_tile * LANES)
        flipped = jnp.transpose(v_first[:, lane(h)] if first == 0 else v_rest[h // some, :, lane(h % some)])
        values_t[h, :, at] = flipped * spread_rows(col, h, first, last_tile)
        dec[lane(i), at] = flipped * spread_rows(tail, h, first, last_tile)

    def sum_main(g):
        found = jnp.dot(dec[lane(g, some * LANES), LANES:rows], maps[LANES:rows, lane(0)], preferred_element_type=F32)
        for u in range(some):
            agg[g * some + u] = found[u * LANES : (u + 1) * LANES]

    for i in range(1, cut + 1):
        if i < cut:
            xload(i).wait()
        for u in range(some):
            h = (i - 1) * some + u
            turn(h, h, 1, tiles)
        if i < cut:
            convolve_group(i)
        sum_main(i - 1)
        if i == 1:
            span_step(0)

    span_step(1)

    @pl.when(me > 0)
    def _():
        halo_copy.wait_recv()

    for j in range(width // LANES):
        edge[j, 0:8, :] = jnp.where(me == 0, 0.0, halo[:, lane(j)].astype(F32)[PACK - 8 :])
        edge[j, 8 : 8 + PACK, :] = xbc[0:PACK, lane(j)].astype(F32)
        done = activate(edge, j, 8, PACK, lane(j))
        if j < heads:
            v_first[0:PACK, lane(j)] = done
        else:
            maps[0:PACK, lane(j - heads)] = done

    def chunk(o):
        return (1 - side) * own + o if o < own else side * own + o - own

    def state(some):
        which = [start + chunk(o) for o in some for start in (theirs, mine)]
        base = 2 * some[0]
        for i, h in enumerate(which):
            turn(h, base + i, 0, 1)
        found = jnp.dot(
            dec[base * LANES : (base + len(which)) * LANES, 0:LANES], maps[0:LANES, lane(0)], preferred_element_type=F32
        )
        for i, h in enumerate(which):
            st = agg[h] + found[i * LANES : (i + 1) * LANES]
            agg[h] = st
            send[0, h] = st.astype(BF16)

    def part(start, o, n):
        if n == half:
            return pl.ds(start, half)
        return pl.ds(start + chunk(o), n)

    def side_of(o):
        return 1 - side if o < own else side

    def to_theirs(o, n=1):
        at = part(theirs, o, n)
        return remote(send.at[0, at], node.at[0, at], chip_send.at[0], chip_recv.at[side_of(o)], mate(0))

    def from_mate(o):
        at = part(mine, o, own)
        return remote(send.at[0, at], node.at[0, at], chip_send.at[0], chip_recv.at[side_of(o)], mate(0))

    def to_mine(o, n=1, start=mine):
        at = part(start, o, n)
        return remote(send.at[0, at], node.at[0, at], chip_send.at[1], chip_recv.at[2 + side_of(o)], mate(0))

    def step_copy(k, o, n=1):
        at = part(mine, o, n)
        if k == 1:
            s, r = step_send.at[o // own], step_recv.at[0 if n > 1 else chunk(o)]
        else:
            s, r = step_send.at[k], step_recv.at[half + (k - 2) * own + o - own]
        return remote(send.at[k, at], node.at[k, at], s, r, mate(k))

    def last_copy(o, hops=1, n=1, source=send):
        at = part(mine, o, n)
        to = lax.rem(me + hops * reach, count)
        return remote(source.at[last, at], node.at[last, at], last_send.at[hops - 1], last_recv.at[o - own], to)

    passed = own // 4

    def last_start(o):
        if o >= own + passed:
            last_copy(o, 2).start()
        last_copy(o).start()

    def x_forward(k, o, n=1):
        at = part(mine, o, n)
        return remote(node.at[k, at], node.at[k, at], xf_send.at[k - 2], xf_recv.at[(k - 2) * own + o % own], mate(1))

    def c_forward(k, o, n=1, start=mine):
        at = part(start, o, n)
        return remote(node.at[k, at], node.at[k, at], cf_send.at[k - 1], cf_recv.at[2 * (k - 1) + side_of(o)], mate(0))

    def combine(k, c):
        h = mine + c
        joined = agg[h] * factor[0, k, pl.ds(h, 1), :] + node[k, h].astype(F32) * factor[1, k, pl.ds(h, 1), :]
        agg[h] = joined
        send[k + 1, h] = joined.astype(BF16)

    def both_ways(k):
        return k < last - 1

    def sends(k, go):
        if both_ways(k):
            go()
        else:
            pl.when(bit_at(k) == 0)(go)

    def join_chip(which):
        from_mate(which[0]).wait_recv()
        for o in which:
            combine(0, chunk(o))
        if which[0] < own:
            for o in which:
                step_copy(1, o).start()
        else:
            @pl.when(side == 0)
            def _():
                for o in which:
                    step_copy(1, o).start()

    def join_x(o):
        step_copy(1, o).wait_recv()

        @pl.when(side == 1)
        def _():
            c_forward(1, o).start()

        combine(1, chunk(o))
        if last == 2:
            @pl.when(quarter == 1)
            def _():
                last_start(o)
        else:
            sends(2, lambda: step_copy(2, o).start())

    def take_x(o):
        @pl.when(side == 1)
        def _():
            step_copy(1, o).wait_recv()
            c_forward(1, o).start()

    def join(k, o):
        if both_ways(k):
            step_copy(k, o).wait_recv()

        @pl.when(bit_at(k) == 1)
        def _():
            if not both_ways(k):
                step_copy(k, o).wait_recv()
            x_forward(k, o).start()
            c_forward(k, o).start()

        if k + 1 < last:
            combine(k, chunk(o))
            sends(k + 1, lambda: step_copy(k + 1, o).start())
        else:
            @pl.when(quarter == 1)
            def _():
                combine(k, chunk(o))
                last_start(o)

    def take(k, o):
        @pl.when(bit_at(k) == 1)
        def _():
            x_forward(k, o).wait_recv()
            c_forward(k, o).start()

    def join_last(o):
        @pl.when(quarter >= 2)
        def _():
            last_copy(o).wait_recv()

        if o < own + passed:
            @pl.when(quarter == 2)
            def _():
                last_copy(o, source=node).start()

        @pl.when(quarter >= 2)
        def _():
            x_forward(last, o).start()
            c_forward(last, o).start()

    for o in range(0, half, 2):
        state((o, o + 1))
    for o in range(half):
        to_theirs(o).start()

    @pl.when(core == 0)
    def _():
        for o in range(half):
            to_mine(o).start()

    join_chip(range(own))
    join_chip(range(own, half))

    late[0].wait()
    late[1].wait()
    lows = []
    for a in range(tiles):
        low = jnp.exp(ll[a] - mids[a])
        for l in range(tile_bits + 1):
            diag[l, :, lane(a)] = lw[l, :, lane(a)] * low
        for b in range(a):
            level = tile_bits + (a ^ b).bit_length()
            cross[a * (a - 1) // 2 + b] = lw[level, :, lane(a)] * jnp.exp(ll[a] - mids[b])
    out_map_t[...] = jnp.transpose(maps[:, lane(1)])
    s_all = lax.broadcasted_iota(jnp.int32, (LANES, LANES), 0)
    t_all = lax.broadcasted_iota(jnp.int32, (LANES, LANES), 1)
    for b in range(tiles):
        scored = jnp.dot(maps[lane(b), lane(0)], out_map_t[...], preferred_element_type=F32)
        for a in range(b, tiles):
            piece = scored[:, a * LANES : (a + 1) * LANES]
            scores_t[lane(b), lane(a)] = (jnp.where(s_all <= t_all, piece, 0.0) if a == b else piece).astype(BF16)
    flipped_gain = jnp.transpose(jnp.concatenate([gain[...], jnp.zeros((LANES - heads, LANES), F32)], axis=0))
    for h in range(heads):
        gain_col[h] = jnp.broadcast_to(flipped_gain[:, h : h + 1], (LANES, LANES))

    def far_table(k):
        level = local_bits + 1 + k
        for a in range(tiles):
            factor = lw[level, :, lane(a)] * jnp.exp(ll[a] + prefix[k])
            far_row[k, :, lane(a)] = jnp.where(bit_at(k) == 1, factor, 0.0)

    t_in = lax.broadcasted_iota(jnp.int32, (PACK, LANES), 1)
    s_in = lax.broadcasted_iota(jnp.int32, (PACK, LANES), 0)
    fine_bits = PACK.bit_length() - 1
    differ = jnp.bitwise_xor(s_in, jnp.bitwise_and(t_in, PACK - 1))
    t_group = lax.shift_right_logical(t_in, fine_bits)
    groups16 = LANES // PACK
    for u in range(wt.shape[0]):
        for a in range(0, tiles, 2):
            wt[u, lane(a + 1), lane(a)] = jnp.zeros((LANES, LANES), BF16)

    def spread(k, h, u):
        row = packed(far_row[k, pl.ds(h, 1), :])
        for s in range(groups16):
            at = k * LANES + s * PACK
            fw[u, at : at + PACK, :] = out_map_t[s * PACK : (s + 1) * PACK, :] * row

    def weights(h, u):
        for a in range(tiles):
            row = [diag[l, pl.ds(h, 1), lane(a)] for l in range(tile_bits + 1)]
            fine = row[fine_bits]
            for l in range(fine_bits - 1, 0, -1):
                fine = jnp.where(differ < (1 << l), row[l], fine)
            fine = jnp.where(differ == 0, row[0], fine).astype(BF16)
            wide = [packed(r) for r in row[fine_bits + 1 :]]
            for j in range(groups16):
                apart = jnp.bitwise_xor(t_group, j)
                chosen = fine
                for l in range(len(wide)):
                    if any((1 << l) <= (x ^ j) < (2 << l) for x in range(j, groups16)):
                        chosen = jnp.where((apart >= (1 << l)) & (apart < (2 << l)), wide[l], chosen)
                at = a * LANES + j * PACK
                wt[u, at : at + PACK, lane(a)] = chosen * scores_t[at : at + PACK, lane(a)]
            for b in range(a):
                row = packed(cross[a * (a - 1) // 2 + b, pl.ds(h, 1), :])
                for j in range(groups16):
                    at = b * LANES + j * PACK
                    wt[u, at : at + PACK, lane(a)] = row * scores_t[at : at + PACK, lane(a)]

    def held(k, h):
        source = node[k, h]
        return jnp.where(bit_at(k) == 1, source, jnp.zeros_like(source))

    def near(first, n):
        for u in range(n):
            weights(first + u, u)
        for u in range(n):
            h = first + u
            for a in range(0, tiles, 2):
                deep = (a + 2) * LANES
                near_t[h, :, a * LANES : deep] = jnp.dot(
                    values_t[h, :, 0:deep], wt[u, 0:deep, a * LANES : deep], preferred_element_type=F32
                )

    def far(h, u, low, high):
        left = jnp.concatenate([held(k, h) for k in range(low, high)], axis=1)
        return jnp.dot(left, fw[u, low * LANES : high * LANES, :], preferred_element_type=F32)

    def add_lower(first, n):
        for u in range(n):
            for k in range(last):
                spread(k, first + u, u)
        for u in range(n):
            near_t[first + u] += far(first + u, u, 0, last)

    def finish(first, n):
        for u in range(n):
            spread(last, first + u, u)
        for u in range(n):
            h = first + u
            mixed = near_t[h] + far(h, u, last, seq_bits)
            mean = jnp.mean(mixed * mixed, axis=0, keepdims=True)
            scaled = mixed * lax.rsqrt(mean + 1e-05) * jnp.concatenate([gain_col[h]] * tiles, axis=1)
            out[:, lane(h)] = jnp.transpose(scaled.astype(BF16))

    def finish_mine(o):
        finish(mine + chunk(o), own)

    def lower_mine(o):
        add_lower(mine + chunk(o), own)

    def lower_theirs(o):
        @pl.when(core == 1)
        def _():
            to_mine(o, own, theirs).wait_recv()

        for k in range(1, last):
            @pl.when(bit_at(k) == 1)
            def _():
                c_forward(k, o, own, theirs).wait_recv()

        add_lower(theirs + chunk(o), own)

    def finish_theirs(o):
        @pl.when(quarter >= 2)
        def _():
            c_forward(last, o, own, theirs).wait_recv()

        finish(theirs + chunk(o), own)

    def take_last(o):
        @pl.when(quarter >= 2)
        def _():
            x_forward(last, o).wait_recv()
            c_forward(last, o).start()

    batch = wt.shape[0]
    far_table(0)
    far_table(1)
    other, kept = range(own), range(own, half)
    near(0, batch)
    near(batch, batch)
    for o in kept:
        join_x(o)
    near(2 * batch, batch)
    if last > 2:
        span_step(2)
    for k in range(2, last):
        if k > 2:
            span_step(k)
        far_table(k)
        for o in kept:
            join(k, o)
        if k == 2:
            for o in other:
                take_x(o)
            near(3 * batch, batch)
        if k < last - 1:
            for o in other:
                take(k, o)
    far_table(last)
    lower_mine(own)
    lower_theirs(own)
    for o in kept:
        join_last(o)
    if last > 2:
        for o in other:
            take(last - 1, o)
    lower_mine(0)
    lower_theirs(0)
    finish_mine(own)
    finish_theirs(own)
    for o in other:
        take_last(o)
    finish_mine(0)
    finish_theirs(0)

    @pl.when(me < count - 1)
    def _():
        halo_copy.wait_send()

    for k in range(last):
        span_copy(k).wait_send()
    to_theirs(0, half).wait_send()
    step_copy(1, 0, own).wait_send()

    @pl.when(core == 0)
    def _():
        to_mine(0, half).wait_send()

    @pl.when(side == 0)
    def _():
        step_copy(1, own, own).wait_send()

    @pl.when(side == 1)
    def _():
        c_forward(1, 0, half).wait_send()

    for k in range(2, last):
        sends(k, lambda: step_copy(k, own, own).wait_send())

        @pl.when(bit_at(k) == 1)
        def _():
            x_forward(k, own, own).wait_send()
            c_forward(k, 0, half).wait_send()

    @pl.when(quarter == 1)
    def _():
        last_copy(own, 1, own).wait_send()
        last_copy(own + passed, 2, own - passed).wait_send()

    @pl.when(quarter == 2)
    def _():
        last_copy(own, 1, passed, node).wait_send()

    @pl.when(quarter >= 2)
    def _():
        x_forward(last, own, own).wait_send()
        c_forward(last, 0, half).wait_send()


def on_device(xbc, conv_weight, log_decay, level_weights, gain):
    rows, width = xbc.shape
    heads = log_decay.shape[0]
    inner = gain.shape[0]
    dim = inner // heads
    tiles = rows // LANES
    levels = level_weights.shape[1]
    seq_bits = lax.axis_size("seq").bit_length() - 1
    last = seq_bits - 1
    dma = pltpu.SemaphoreType.DMA
    hbm = pl.BlockSpec(memory_space=pltpu.HBM)
    square = (heads, dim, LANES)
    return pl.pallas_call(
        functools.partial(kernel, seq_bits),
        out_shape=pltpu.VMEM((rows, inner), BF16),
        in_specs=[hbm] * 5,
        out_specs=pl.BlockSpec(memory_space=pltpu.VMEM),
        scratch_shapes=[
            pltpu.VMEM((rows, width), BF16),
            pltpu.VMEM(conv_weight.shape, F32),
            pltpu.VMEM((heads, rows), F32),
            pltpu.VMEM((levels, heads, rows), F32),
            pltpu.VMEM((heads, dim), F32),
            dma((9,)),
            pltpu.VMEM((heads // 2, rows + 8, LANES), F32),
            pltpu.VMEM((width // LANES, PACK + 8, LANES), F32),
            pltpu.VMEM((PACK, width), BF16),
            pltpu.VMEM((LANES, inner), BF16),
            pltpu.VMEM((4, rows - LANES, inner // 4), BF16),
            pltpu.VMEM((rows, width - inner), BF16),
            pltpu.VMEM((LANES, rows), BF16),
            pltpu.VMEM((heads, dim, rows), BF16),
            pltpu.VMEM((heads * dim, rows), BF16),
            pltpu.VMEM((heads, rows), F32),
            pltpu.VMEM((heads, rows), F32),
            pltpu.VMEM((LANES.bit_length(), heads, rows), F32),
            pltpu.VMEM((tiles * (tiles - 1) // 2, heads, LANES), F32),
            pltpu.VMEM((seq_bits, heads, rows), F32),
            pltpu.VMEM((rows, rows), BF16),
            pltpu.VMEM((heads // 4, rows, rows), BF16),
            pltpu.VMEM((heads // 4, seq_bits * LANES, rows), BF16),
            pltpu.VMEM((heads, dim, rows), F32),
            pltpu.VMEM(square, F32),
            pltpu.VMEM(square, F32),
            pltpu.VMEM((seq_bits,) + square, BF16),
            pltpu.VMEM((seq_bits,) + square, BF16),
            pltpu.VMEM((seq_bits + 1, heads, LANES), F32),
            pltpu.VMEM((seq_bits, heads, LANES), F32),
            pltpu.VMEM((seq_bits + 1, heads, LANES), F32),
            pltpu.VMEM((2, seq_bits, heads, LANES), F32),
            dma((2,)),
            dma((last,)),
            dma((last,)),
            dma((2,)),
            dma((4,)),
            dma((last,)),
            dma((heads // 2 + (last - 2) * heads // 4,)),
            dma((2,)),
            dma((heads // 4,)),
            dma((last - 1,)),
            dma(((last - 1) * heads // 4,)),
            dma((last,)),
            dma((2 * last,)),
        ],
        compiler_params=pltpu.CompilerParams(
            collective_id=0, has_side_effects=True, vmem_limit_bytes=61 * 1024 * 1024
        ),
        name="mixer",
    )(xbc, conv_weight, log_decay, level_weights.transpose(1, 0, 2), gain.reshape(heads, dim))


def solution(mesh):
    in_specs = (
        P(("groups", "seq"), None),
        P(),
        P(None, ("groups", "seq")),
        P(None, None, ("groups", "seq")),
        P(),
    )
    out_specs = P(("groups", "seq"), None)
    return jax.shard_map(
        on_device, mesh=mesh, in_specs=in_specs, out_specs=out_specs, check_vma=False
    )
```

```python
import functools
import jax
import jax.numpy as jnp
from jax import lax
from jax.experimental import pallas as pl
from jax.experimental.pallas import tpu as pltpu
from jax.sharding import PartitionSpec as P

LANES = 128
PACK = 16
MESH = pl.DeviceIdType.MESH
F32, BF16 = jnp.float32, jnp.bfloat16


def lane(i, width=LANES):
    if isinstance(i, int):
        return pl.ds(i * width, width)
    return pl.ds(pl.multiple_of(i * width, LANES), width)


def packed(row, times=1):
    return jnp.broadcast_to(row, (PACK * times, row.shape[1])).astype(BF16)


def kernel(
    seq_bits, xbc_hbm, taps_hbm, decay_hbm, lw_hbm, gain_hbm, out,
    xbc, taps, decay, lw, gain, load_sem, pad, edge, halo, v_first, v_rest, maps, out_map_t, values_t, dec,
    tail, col, diag, cross, far_row, scores_t, wt, fw, near_t, gain_col,
    agg, send, node, span, span_rx, prefix, factor,
    halo_sem, span_send, span_recv, chip_send, chip_recv, step_send, step_recv, last_send, last_recv, xf_send, xf_recv, cf_send, cf_recv,
):
    rows, width = xbc.shape
    heads = decay.shape[0]
    kern = taps.shape[0]
    half = heads // 2
    own = half // 2
    tiles = rows // LANES
    tile_bits = LANES.bit_length() - 1
    local_bits = rows.bit_length() - 1
    count = 1 << seq_bits
    last = seq_bits - 1
    me = lax.axis_index("seq")
    group = lax.axis_index("groups")
    core = lax.rem(me, 2)
    side = lax.rem(lax.div(me, 2), 2)
    after, before = lax.rem(me + 1, count), lax.rem(me + count - 1, count)
    reach = count // 4
    quarter = lax.div(me, reach)
    ahead = lax.rem(me + reach, count)
    mine, theirs = core * half, (1 - core) * half

    def bit_at(k):
        return lax.rem(lax.div(me, 1 << k), 2)

    def mate(k):
        return me + (1 - 2 * bit_at(k)) * (1 << k)

    def remote(src, dst, s, r, to):
        return pltpu.make_async_remote_copy(
            src_ref=src, dst_ref=dst, send_sem=s, recv_sem=r,
            device_id=(group, to), device_id_type=MESH,
        )

    cut = 4
    some = heads // cut
    loads = [pltpu.make_async_copy(decay_hbm, decay, load_sem.at[0]), pltpu.make_async_copy(taps_hbm, taps, load_sem.at[1])]

    def xload(i):
        at = pl.ds(heads * LANES, width - heads * LANES) if i is None else lane(i, some * LANES)
        return pltpu.make_async_copy(xbc_hbm.at[:, at], xbc.at[:, at], load_sem.at[2 + cut if i is None else 2 + i])

    xloads = [xload(None)] + [xload(i) for i in range(cut)]
    late = [pltpu.make_async_copy(lw_hbm, lw, load_sem.at[3 + cut]), pltpu.make_async_copy(gain_hbm, gain, load_sem.at[4 + cut])]
    for load in loads + xloads + late:
        load.start()
    barrier = pltpu.get_barrier_semaphore()
    partners = [
        (me < count - 1, after), (me > 0, before),
        (quarter == 1, ahead), (quarter == 1, lax.rem(me + 2 * reach, count)),
        (quarter >= 2, lax.rem(me + count - (quarter - 1) * reach, count)),
    ] + [(None, mate(k)) for k in range(last)]
    expected = 0
    for there, to in partners:
        def greet():
            pl.semaphore_signal(barrier, inc=1, device_id=(group, to), device_id_type=MESH)

        if there is None:
            greet()
            expected = expected + 1
        else:
            pl.when(there)(greet)
            expected = expected + there.astype(jnp.int32)
    tri = (
        lax.broadcasted_iota(jnp.int32, (LANES, LANES), 0)
        <= lax.broadcasted_iota(jnp.int32, (LANES, LANES), 1)
    ).astype(F32).astype(BF16)
    loads[0].wait()
    rest = jnp.concatenate([decay[:, lane(a)] for a in range(tiles)], axis=0)
    parts = []
    for _ in range(3):
        part = rest.astype(BF16)
        rest = rest - part.astype(F32)
        parts.append(part)
    sums = jnp.dot(jnp.concatenate(parts, axis=0), tri, preferred_element_type=F32)
    step = tiles * heads
    sums = sums[2 * step : 3 * step] + sums[step : 2 * step] + sums[0:step]
    ll, base = [], jnp.zeros((heads, LANES), F32)
    for a in range(tiles):
        ll.append(sums[a * heads : (a + 1) * heads] + base)
        base = jnp.broadcast_to(ll[a][:, LANES - 1 :], (heads, LANES))
    total = base
    span[0] = total

    pad[:, 0:8, :] = jnp.zeros((pad.shape[0], 8, LANES), F32)
    loads[1].wait()

    def activate(ref, lead, first, n, at):
        weights = taps[:, at] * 0.5
        start = first - kern + 1
        total = ref[lead, start : start + n, :] * weights[0:1]
        for k in range(1, kern):
            total = total + ref[lead, start + k : start + k + n, :] * weights[k : k + 1]
        return (total * jnp.tanh(total) + total).astype(BF16)

    def convolve(j, u):
        pad[u, 8 : 8 + rows, :] = xbc[:, lane(j)].astype(F32)
        return activate(pad, u, 8, rows, lane(j))

    xloads[0].wait()
    for u in range(width // LANES - heads):
        maps[:, lane(u)] = convolve(heads + u, u)

    def convolve_group(i):
        for u in range(some):
            done = convolve(i * some + u, i % 2 * some + u)
            v_first[:, lane(i * some + u)] = done[0:LANES]
            v_rest[i, :, lane(u)] = done[LANES:rows]

    pl.semaphore_wait(barrier, expected)
    halo_copy = remote(xbc_hbm.at[rows - PACK : rows, :], halo, halo_sem.at[0], halo_sem.at[1], after)

    @pl.when(me < count - 1)
    def _():
        halo_copy.start()


    def span_copy(k):
        return remote(span.at[k], span_rx.at[k], span_send.at[k], span_recv.at[k], mate(k))

    span_copy(0).start()

    mids = [jnp.broadcast_to(x[:, LANES // 2 - 1 : LANES // 2], (heads, LANES)) for x in ll]
    for a in range(tiles):
        tail[:, lane(a)] = jnp.exp(total - ll[a])
        col[:, lane(a)] = jnp.exp(mids[a] - ll[a])

    def span_step(k):
        span_copy(k).wait_recv()
        other = span_rx[k]
        upper = bit_at(k) == 1
        prefix[k + 1] = prefix[k] + jnp.where(upper, other, 0.0)
        keep = jnp.exp(jnp.where(upper, span[k], other))
        factor[0, k] = jnp.where(upper, 1.0, keep)
        factor[1, k] = jnp.where(upper, keep, 1.0)
        span[k + 1] = span[k] + other
        if k + 1 < last:
            span_copy(k + 1).start()

    prefix[0] = jnp.zeros((heads, LANES), F32)
    xload(0).wait()
    convolve_group(0)

    def spread_rows(ref, h, first, last_tile):
        row = packed(ref[pl.ds(h, 1), :][:, first * LANES : last_tile * LANES])
        return jnp.concatenate([row] * (LANES // PACK), axis=0)

    def turn(h, i, first, last_tile):
        at = slice(first * LANES, last_tile * LANES)
        flipped = jnp.transpose(v_first[:, lane(h)] if first == 0 else v_rest[h // some, :, lane(h % some)])
        values_t[h, :, at] = flipped * spread_rows(col, h, first, last_tile)
        dec[lane(i), at] = flipped * spread_rows(tail, h, first, last_tile)

    def sum_main(g):
        found = jnp.dot(dec[lane(g, some * LANES), LANES:rows], maps[LANES:rows, lane(0)], preferred_element_type=F32)
        for u in range(some):
            agg[g * some + u] = found[u * LANES : (u + 1) * LANES]

    for i in range(1, cut + 1):
        if i < cut:
            xload(i).wait()
        for u in range(some):
            h = (i - 1) * some + u
            turn(h, h, 1, tiles)
        if i < cut:
            convolve_group(i)
        sum_main(i - 1)
        if i == 1:
            span_step(0)


    @pl.when(me > 0)
    def _():
        halo_copy.wait_recv()

    for j in range(width // LANES):
        edge[j, 0:8, :] = jnp.where(me == 0, 0.0, halo[:, lane(j)].astype(F32)[PACK - 8 :])
        edge[j, 8 : 8 + PACK, :] = xbc[0:PACK, lane(j)].astype(F32)
        done = activate(edge, j, 8, PACK, lane(j))
        if j < heads:
            v_first[0:PACK, lane(j)] = done
        else:
            maps[0:PACK, lane(j - heads)] = done

    def chunk(o):
        return (1 - side) * own + o if o < own else side * own + o - own

    def state(some):
        which = [start + chunk(o) for o in some for start in (theirs, mine)]
        base = 2 * some[0]
        for i, h in enumerate(which):
            turn(h, base + i, 0, 1)
        found = jnp.dot(
            dec[base * LANES : (base + len(which)) * LANES, 0:LANES], maps[0:LANES, lane(0)], preferred_element_type=F32
        )
        for i, h in enumerate(which):
            st = agg[h] + found[i * LANES : (i + 1) * LANES]
            agg[h] = st
            send[0, h] = st.astype(BF16)

    def part(start, o, n):
        if n == half:
            return pl.ds(start, half)
        return pl.ds(start + chunk(o), n)

    def side_of(o):
        return 1 - side if o < own else side

    def to_theirs(o, n=1):
        at = part(theirs, o, n)
        return remote(send.at[0, at], node.at[0, at], chip_send.at[0], chip_recv.at[side_of(o)], mate(0))

    def from_mate(o):
        at = part(mine, o, own)
        return remote(send.at[0, at], node.at[0, at], chip_send.at[0], chip_recv.at[side_of(o)], mate(0))

    def to_mine(o, n=1, start=mine):
        at = part(start, o, n)
        return remote(send.at[0, at], node.at[0, at], chip_send.at[1], chip_recv.at[2 + side_of(o)], mate(0))

    def step_copy(k, o, n=1):
        at = part(mine, o, n)
        if k == 1:
            s, r = step_send.at[o // own], step_recv.at[0 if n > 1 else chunk(o)]
        else:
            s, r = step_send.at[k], step_recv.at[half + (k - 2) * own + o - own]
        return remote(send.at[k, at], node.at[k, at], s, r, mate(k))

    def last_copy(o, hops=1, n=1, source=send):
        at = part(mine, o, n)
        to = lax.rem(me + hops * reach, count)
        return remote(source.at[last, at], node.at[last, at], last_send.at[hops - 1], last_recv.at[o - own], to)

    passed = own // 4

    def last_start(o):
        if o >= own + passed:
            last_copy(o, 2).start()
        last_copy(o).start()

    def x_forward(k, o, n=1):
        at = part(mine, o, n)
        return remote(node.at[k, at], node.at[k, at], xf_send.at[k - 2], xf_recv.at[(k - 2) * own + o % own], mate(1))

    def c_forward(k, o, n=1, start=mine):
        at = part(start, o, n)
        return remote(node.at[k, at], node.at[k, at], cf_send.at[k - 1], cf_recv.at[2 * (k - 1) + side_of(o)], mate(0))

    def combine(k, c):
        h = mine + c
        joined = agg[h] * factor[0, k, pl.ds(h, 1), :] + node[k, h].astype(F32) * factor[1, k, pl.ds(h, 1), :]
        agg[h] = joined
        send[k + 1, h] = joined.astype(BF16)

    def both_ways(k):
        return k < last - 1

    def sends(k, go):
        if both_ways(k):
            go()
        else:
            pl.when(bit_at(k) == 0)(go)

    def join_chip(which):
        from_mate(which[0]).wait_recv()
        for o in which:
            combine(0, chunk(o))
        if which[0] < own:
            for o in which:
                step_copy(1, o).start()
        else:
            @pl.when(side == 0)
            def _():
                for o in which:
                    step_copy(1, o).start()

    def join_x(o):
        step_copy(1, o).wait_recv()

        @pl.when(side == 1)
        def _():
            c_forward(1, o).start()

        combine(1, chunk(o))
        if last == 2:
            @pl.when(quarter == 1)
            def _():
                last_start(o)
        else:
            sends(2, lambda: step_copy(2, o).start())

    def take_x(o):
        @pl.when(side == 1)
        def _():
            step_copy(1, o).wait_recv()
            c_forward(1, o).start()

    def join(k, o):
        if both_ways(k):
            step_copy(k, o).wait_recv()

        @pl.when(bit_at(k) == 1)
        def _():
            if not both_ways(k):
                step_copy(k, o).wait_recv()
            x_forward(k, o).start()
            c_forward(k, o).start()

        if k + 1 < last:
            combine(k, chunk(o))
            sends(k + 1, lambda: step_copy(k + 1, o).start())
        else:
            @pl.when(quarter == 1)
            def _():
                combine(k, chunk(o))
                last_start(o)

    def take(k, o):
        @pl.when(bit_at(k) == 1)
        def _():
            x_forward(k, o).wait_recv()
            c_forward(k, o).start()

    def share_last(o):
        last_copy(o).wait_recv()
        x_forward(last, o).start()
        c_forward(last, o).start()

    def join_last():
        direct = range(own + passed, half)

        @pl.when(quarter == 2)
        def _():
            for o in range(own, own + passed):
                last_copy(o).wait_recv()
                last_copy(o, source=node).start()
                x_forward(last, o).start()
                c_forward(last, o).start()
            for o in direct:
                share_last(o)

        @pl.when(quarter == 3)
        def _():
            for o in direct:
                share_last(o)
            for o in range(own, own + passed):
                share_last(o)

    for some_heads in (range(own), range(own, half)):
        for o in some_heads[::2]:
            state((o, o + 1))
        for o in some_heads:
            to_theirs(o).start()

    @pl.when(core == 0)
    def _():
        for o in range(half):
            to_mine(o).start()

    join_chip(range(own))
    join_chip(range(own, half))
    span_step(1)

    late[0].wait()
    late[1].wait()
    lows = []
    for a in range(tiles):
        low = jnp.exp(ll[a] - mids[a])
        for l in range(tile_bits + 1):
            diag[l, :, lane(a)] = lw[l, :, lane(a)] * low
        for b in range(a):
            level = tile_bits + (a ^ b).bit_length()
            cross[a * (a - 1) // 2 + b] = lw[level, :, lane(a)] * jnp.exp(ll[a] - mids[b])
    out_map_t[...] = jnp.transpose(maps[:, lane(1)])
    s_all = lax.broadcasted_iota(jnp.int32, (LANES, LANES), 0)
    t_all = lax.broadcasted_iota(jnp.int32, (LANES, LANES), 1)
    for b in range(tiles):
        scored = jnp.dot(maps[lane(b), lane(0)], out_map_t[...], preferred_element_type=F32)
        for a in range(b, tiles):
            piece = scored[:, a * LANES : (a + 1) * LANES]
            scores_t[lane(b), lane(a)] = (jnp.where(s_all <= t_all, piece, 0.0) if a == b else piece).astype(BF16)
    flipped_gain = jnp.transpose(jnp.concatenate([gain[...], jnp.zeros((LANES - heads, LANES), F32)], axis=0))
    for h in range(heads):
        gain_col[h] = jnp.broadcast_to(flipped_gain[:, h : h + 1], (LANES, LANES))

    def far_table(k):
        level = local_bits + 1 + k
        for a in range(tiles):
            factor = lw[level, :, lane(a)] * jnp.exp(ll[a] + prefix[k])
            far_row[k, :, lane(a)] = jnp.where(bit_at(k) == 1, factor, 0.0)

    t_in = lax.broadcasted_iota(jnp.int32, (PACK, LANES), 1)
    s_in = lax.broadcasted_iota(jnp.int32, (PACK, LANES), 0)
    fine_bits = PACK.bit_length() - 1
    differ = jnp.bitwise_xor(s_in, jnp.bitwise_and(t_in, PACK - 1))
    t_group = lax.shift_right_logical(t_in, fine_bits)
    groups16 = LANES // PACK
    for u in range(wt.shape[0]):
        for a in range(0, tiles, 2):
            wt[u, lane(a + 1), lane(a)] = jnp.zeros((LANES, LANES), BF16)

    def spread(k, h, u):
        row = packed(far_row[k, pl.ds(h, 1), :])
        for s in range(groups16):
            at = k * LANES + s * PACK
            fw[u, at : at + PACK, :] = out_map_t[s * PACK : (s + 1) * PACK, :] * row

    def weights(h, u):
        for a in range(tiles):
            row = [diag[l, pl.ds(h, 1), lane(a)] for l in range(tile_bits + 1)]
            fine = row[fine_bits]
            for l in range(fine_bits - 1, 0, -1):
                fine = jnp.where(differ < (1 << l), row[l], fine)
            fine = jnp.where(differ == 0, row[0], fine).astype(BF16)
            wide = [packed(r) for r in row[fine_bits + 1 :]]
            for j in range(groups16):
                apart = jnp.bitwise_xor(t_group, j)
                chosen = fine
                for l in range(len(wide)):
                    if any((1 << l) <= (x ^ j) < (2 << l) for x in range(j, groups16)):
                        chosen = jnp.where((apart >= (1 << l)) & (apart < (2 << l)), wide[l], chosen)
                at = a * LANES + j * PACK
                wt[u, at : at + PACK, lane(a)] = chosen * scores_t[at : at + PACK, lane(a)]
            for b in range(a):
                row = packed(cross[a * (a - 1) // 2 + b, pl.ds(h, 1), :])
                for j in range(groups16):
                    at = b * LANES + j * PACK
                    wt[u, at : at + PACK, lane(a)] = row * scores_t[at : at + PACK, lane(a)]

    def held(k, h):
        source = node[k, h]
        return jnp.where(bit_at(k) == 1, source, jnp.zeros_like(source))

    def near(first, n):
        for u in range(n):
            weights(first + u, u)
        for u in range(n):
            h = first + u
            for a in range(0, tiles, 2):
                deep = (a + 2) * LANES
                near_t[h, :, a * LANES : deep] = jnp.dot(
                    values_t[h, :, 0:deep], wt[u, 0:deep, a * LANES : deep], preferred_element_type=F32
                )

    def far(h, u, low, high):
        left = jnp.concatenate([held(k, h) for k in range(low, high)], axis=1)
        return jnp.dot(left, fw[u, low * LANES : high * LANES, :], preferred_element_type=F32)

    def add_lower(first, n):
        for u in range(n):
            for k in range(last):
                spread(k, first + u, u)
        for u in range(n):
            near_t[first + u] += far(first + u, u, 0, last)

    def finish(first, n):
        for u in range(n):
            spread(last, first + u, u)
        for u in range(n):
            h = first + u
            mixed = near_t[h] + far(h, u, last, seq_bits)
            mean = jnp.mean(mixed * mixed, axis=0, keepdims=True)
            scaled = mixed * lax.rsqrt(mean + 1e-05) * jnp.concatenate([gain_col[h]] * tiles, axis=1)
            out[:, lane(h)] = jnp.transpose(scaled.astype(BF16))

    def finish_mine(o):
        finish(mine + chunk(o), own)

    def lower_mine(o):
        add_lower(mine + chunk(o), own)

    def lower_theirs(o):
        @pl.when(core == 1)
        def _():
            to_mine(o, own, theirs).wait_recv()

        for k in range(1, last):
            @pl.when(bit_at(k) == 1)
            def _():
                c_forward(k, o, own, theirs).wait_recv()

        add_lower(theirs + chunk(o), own)

    def finish_theirs(o):
        @pl.when(quarter >= 2)
        def _():
            c_forward(last, o, own, theirs).wait_recv()

        finish(theirs + chunk(o), own)

    def take_last(o):
        x_forward(last, o).wait_recv()
        c_forward(last, o).start()

    batch = wt.shape[0]
    far_table(0)
    far_table(1)
    other, kept = range(own), range(own, half)
    near(0, batch)
    near(batch, batch)
    for o in kept:
        join_x(o)
    near(2 * batch, batch)
    if last > 2:
        span_step(2)
    for k in range(2, last):
        if k > 2:
            span_step(k)
        far_table(k)
        for o in kept:
            join(k, o)
        if k == 2:
            for o in other:
                take_x(o)
            near(3 * batch, batch)
        if k < last - 1:
            for o in other:
                take(k, o)
    far_table(last)
    lower_mine(own)
    lower_theirs(own)
    join_last()
    if last > 2:
        for o in other:
            take(last - 1, o)
    lower_mine(0)
    lower_theirs(0)
    finish_mine(own)
    finish_theirs(own)
    @pl.when(quarter == 2)
    def _():
        for o in other:
            take_last(o)

    @pl.when(quarter == 3)
    def _():
        for o in [*other[passed:], *other[:passed]]:
            take_last(o)

    finish_mine(0)
    finish_theirs(0)

    @pl.when(me < count - 1)
    def _():
        halo_copy.wait_send()

    for k in range(last):
        span_copy(k).wait_send()
    to_theirs(0, half).wait_send()
    step_copy(1, 0, own).wait_send()

    @pl.when(core == 0)
    def _():
        to_mine(0, half).wait_send()

    @pl.when(side == 0)
    def _():
        step_copy(1, own, own).wait_send()

    @pl.when(side == 1)
    def _():
        c_forward(1, 0, half).wait_send()

    for k in range(2, last):
        sends(k, lambda: step_copy(k, own, own).wait_send())

        @pl.when(bit_at(k) == 1)
        def _():
            x_forward(k, own, own).wait_send()
            c_forward(k, 0, half).wait_send()

    @pl.when(quarter == 1)
    def _():
        last_copy(own, 1, own).wait_send()
        last_copy(own + passed, 2, own - passed).wait_send()

    @pl.when(quarter == 2)
    def _():
        last_copy(own, 1, passed, node).wait_send()

    @pl.when(quarter >= 2)
    def _():
        x_forward(last, own, own).wait_send()
        c_forward(last, 0, half).wait_send()


def on_device(xbc, conv_weight, log_decay, level_weights, gain):
    rows, width = xbc.shape
    heads = log_decay.shape[0]
    inner = gain.shape[0]
    dim = inner // heads
    tiles = rows // LANES
    levels = level_weights.shape[1]
    seq_bits = lax.axis_size("seq").bit_length() - 1
    last = seq_bits - 1
    dma = pltpu.SemaphoreType.DMA
    hbm = pl.BlockSpec(memory_space=pltpu.HBM)
    square = (heads, dim, LANES)
    return pl.pallas_call(
        functools.partial(kernel, seq_bits),
        out_shape=pltpu.VMEM((rows, inner), BF16),
        in_specs=[hbm] * 5,
        out_specs=pl.BlockSpec(memory_space=pltpu.VMEM),
        scratch_shapes=[
            pltpu.VMEM((rows, width), BF16),
            pltpu.VMEM(conv_weight.shape, F32),
            pltpu.VMEM((heads, rows), F32),
            pltpu.VMEM((levels, heads, rows), F32),
            pltpu.VMEM((heads, dim), F32),
            dma((9,)),
            pltpu.VMEM((heads // 2, rows + 8, LANES), F32),
            pltpu.VMEM((width // LANES, PACK + 8, LANES), F32),
            pltpu.VMEM((PACK, width), BF16),
            pltpu.VMEM((LANES, inner), BF16),
            pltpu.VMEM((4, rows - LANES, inner // 4), BF16),
            pltpu.VMEM((rows, width - inner), BF16),
            pltpu.VMEM((LANES, rows), BF16),
            pltpu.VMEM((heads, dim, rows), BF16),
            pltpu.VMEM((heads * dim, rows), BF16),
            pltpu.VMEM((heads, rows), F32),
            pltpu.VMEM((heads, rows), F32),
            pltpu.VMEM((LANES.bit_length(), heads, rows), F32),
            pltpu.VMEM((tiles * (tiles - 1) // 2, heads, LANES), F32),
            pltpu.VMEM((seq_bits, heads, rows), F32),
            pltpu.VMEM((rows, rows), BF16),
            pltpu.VMEM((heads // 4, rows, rows), BF16),
            pltpu.VMEM((heads // 4, seq_bits * LANES, rows), BF16),
            pltpu.VMEM((heads, dim, rows), F32),
            pltpu.VMEM(square, F32),
            pltpu.VMEM(square, F32),
            pltpu.VMEM((seq_bits,) + square, BF16),
            pltpu.VMEM((seq_bits,) + square, BF16),
            pltpu.VMEM((seq_bits + 1, heads, LANES), F32),
            pltpu.VMEM((seq_bits, heads, LANES), F32),
            pltpu.VMEM((seq_bits + 1, heads, LANES), F32),
            pltpu.VMEM((2, seq_bits, heads, LANES), F32),
            dma((2,)),
            dma((last,)),
            dma((last,)),
            dma((2,)),
            dma((4,)),
            dma((last,)),
            dma((heads // 2 + (last - 2) * heads // 4,)),
            dma((2,)),
            dma((heads // 4,)),
            dma((last - 1,)),
            dma(((last - 1) * heads // 4,)),
            dma((last,)),
            dma((2 * last,)),
        ],
        compiler_params=pltpu.CompilerParams(
            collective_id=0, has_side_effects=True, vmem_limit_bytes=61 * 1024 * 1024
        ),
        name="mixer",
    )(xbc, conv_weight, log_decay, level_weights.transpose(1, 0, 2), gain.reshape(heads, dim))


def solution(mesh):
    in_specs = (
        P(("groups", "seq"), None),
        P(),
        P(None, ("groups", "seq")),
        P(None, None, ("groups", "seq")),
        P(),
    )
    out_specs = P(("groups", "seq"), None)
    return jax.shard_map(
        on_device, mesh=mesh, in_specs=in_specs, out_specs=out_specs, check_vma=False
    )
```

```python
import functools
import jax
import jax.numpy as jnp
from jax import lax
from jax.experimental import pallas as pl
from jax.experimental.pallas import tpu as pltpu
from jax.sharding import PartitionSpec as P

LANES = 128
PACK = 16
MESH = pl.DeviceIdType.MESH
F32, BF16 = jnp.float32, jnp.bfloat16


def lane(i, width=LANES):
    if isinstance(i, int):
        return pl.ds(i * width, width)
    return pl.ds(pl.multiple_of(i * width, LANES), width)


def packed(row, times=1):
    return jnp.broadcast_to(row, (PACK * times, row.shape[1])).astype(BF16)


def kernel(
    seq_bits, xbc_hbm, taps_hbm, decay_hbm, lw_hbm, gain_hbm, out,
    xbc, taps, decay, lw, gain, load_sem, pad, edge, halo, v_first, v_rest, maps, out_map_t, values_t, dec,
    tail, col, diag, cross, far_row, scores_t, wt, fw, near_t, gain_col,
    agg, send, node, span, span_rx, prefix, factor,
    halo_sem, span_send, span_recv, chip_send, chip_recv, step_send, step_recv, last_send, last_recv, xf_send, xf_recv, cf_send, cf_recv,
):
    rows, width = xbc.shape
    heads = decay.shape[0]
    kern = taps.shape[0]
    half = heads // 2
    own = half // 2
    tiles = rows // LANES
    tile_bits = LANES.bit_length() - 1
    local_bits = rows.bit_length() - 1
    count = 1 << seq_bits
    last = seq_bits - 1
    me = lax.axis_index("seq")
    group = lax.axis_index("groups")
    core = lax.rem(me, 2)
    side = lax.rem(lax.div(me, 2), 2)
    after, before = lax.rem(me + 1, count), lax.rem(me + count - 1, count)
    reach = count // 4
    quarter = lax.div(me, reach)
    ahead = lax.rem(me + reach, count)
    mine, theirs = core * half, (1 - core) * half

    def bit_at(k):
        return lax.rem(lax.div(me, 1 << k), 2)

    def mate(k):
        return me + (1 - 2 * bit_at(k)) * (1 << k)

    def remote(src, dst, s, r, to):
        return pltpu.make_async_remote_copy(
            src_ref=src, dst_ref=dst, send_sem=s, recv_sem=r,
            device_id=(group, to), device_id_type=MESH,
        )

    cut = 4
    some = heads // cut
    loads = [pltpu.make_async_copy(decay_hbm, decay, load_sem.at[0]), pltpu.make_async_copy(taps_hbm, taps, load_sem.at[1])]

    def xload(i):
        at = pl.ds(heads * LANES, width - heads * LANES) if i is None else lane(i, some * LANES)
        return pltpu.make_async_copy(xbc_hbm.at[:, at], xbc.at[:, at], load_sem.at[2 + cut if i is None else 2 + i])

    xloads = [xload(None)] + [xload(i) for i in range(cut)]
    late = [pltpu.make_async_copy(lw_hbm, lw, load_sem.at[3 + cut]), pltpu.make_async_copy(gain_hbm, gain, load_sem.at[4 + cut])]
    for load in loads + xloads + late:
        load.start()
    barrier = pltpu.get_barrier_semaphore()
    partners = [
        (me < count - 1, after), (me > 0, before),
        (quarter == 1, ahead), (quarter == 1, lax.rem(me + 2 * reach, count)),
        (quarter >= 2, lax.rem(me + count - (quarter - 1) * reach, count)),
    ] + [(None, mate(k)) for k in range(last)]
    expected = 0
    for there, to in partners:
        def greet():
            pl.semaphore_signal(barrier, inc=1, device_id=(group, to), device_id_type=MESH)

        if there is None:
            greet()
            expected = expected + 1
        else:
            pl.when(there)(greet)
            expected = expected + there.astype(jnp.int32)
    tri = (
        lax.broadcasted_iota(jnp.int32, (LANES, LANES), 0)
        <= lax.broadcasted_iota(jnp.int32, (LANES, LANES), 1)
    ).astype(F32).astype(BF16)
    loads[0].wait()
    rest = jnp.concatenate([decay[:, lane(a)] for a in range(tiles)], axis=0)
    parts = []
    for _ in range(3):
        part = rest.astype(BF16)
        rest = rest - part.astype(F32)
        parts.append(part)
    sums = jnp.dot(jnp.concatenate(parts, axis=0), tri, preferred_element_type=F32)
    step = tiles * heads
    sums = sums[2 * step : 3 * step] + sums[step : 2 * step] + sums[0:step]
    ll, base = [], jnp.zeros((heads, LANES), F32)
    for a in range(tiles):
        ll.append(sums[a * heads : (a + 1) * heads] + base)
        base = jnp.broadcast_to(ll[a][:, LANES - 1 :], (heads, LANES))
    total = base
    span[0] = total

    pad[:, 0:8, :] = jnp.zeros((pad.shape[0], 8, LANES), F32)
    loads[1].wait()

    def activate(ref, lead, first, n, at):
        weights = taps[:, at] * 0.5
        start = first - kern + 1
        total = ref[lead, start : start + n, :] * weights[0:1]
        for k in range(1, kern):
            total = total + ref[lead, start + k : start + k + n, :] * weights[k : k + 1]
        return (total * jnp.tanh(total) + total).astype(BF16)

    def convolve(j, u):
        pad[u, 8 : 8 + rows, :] = xbc[:, lane(j)].astype(F32)
        return activate(pad, u, 8, rows, lane(j))

    xloads[0].wait()
    for u in range(width // LANES - heads):
        maps[:, lane(u)] = convolve(heads + u, u)

    def convolve_group(i):
        for u in range(some):
            done = convolve(i * some + u, i % 2 * some + u)
            v_first[:, lane(i * some + u)] = done[0:LANES]
            v_rest[i, :, lane(u)] = done[LANES:rows]

    pl.semaphore_wait(barrier, expected)
    halo_copy = remote(xbc_hbm.at[rows - PACK : rows, :], halo, halo_sem.at[0], halo_sem.at[1], after)

    @pl.when(me < count - 1)
    def _():
        halo_copy.start()


    def span_copy(k):
        return remote(span.at[k], span_rx.at[k], span_send.at[k], span_recv.at[k], mate(k))

    span_copy(0).start()

    mids = [jnp.broadcast_to(x[:, LANES // 2 - 1 : LANES // 2], (heads, LANES)) for x in ll]
    for a in range(tiles):
        tail[:, lane(a)] = jnp.exp(total - ll[a])
        col[:, lane(a)] = jnp.exp(mids[a] - ll[a])

    def span_step(k):
        span_copy(k).wait_recv()
        other = span_rx[k]
        upper = bit_at(k) == 1
        prefix[k + 1] = prefix[k] + jnp.where(upper, other, 0.0)
        keep = jnp.exp(jnp.where(upper, span[k], other))
        factor[0, k] = jnp.where(upper, 1.0, keep)
        factor[1, k] = jnp.where(upper, keep, 1.0)
        span[k + 1] = span[k] + other
        if k + 1 < last:
            span_copy(k + 1).start()

    prefix[0] = jnp.zeros((heads, LANES), F32)
    xload(0).wait()
    convolve_group(0)

    def spread_rows(ref, h, first, last_tile):
        row = packed(ref[pl.ds(h, 1), :][:, first * LANES : last_tile * LANES])
        return jnp.concatenate([row] * (LANES // PACK), axis=0)

    def turn(h, i, first, last_tile):
        at = slice(first * LANES, last_tile * LANES)
        flipped = jnp.transpose(v_first[:, lane(h)] if first == 0 else v_rest[h // some, :, lane(h % some)])
        values_t[h, :, at] = flipped * spread_rows(col, h, first, last_tile)
        dec[lane(i), at] = flipped * spread_rows(tail, h, first, last_tile)

    def sum_main(g):
        found = jnp.dot(dec[lane(g, some * LANES), LANES:rows], maps[LANES:rows, lane(0)], preferred_element_type=F32)
        for u in range(some):
            agg[g * some + u] = found[u * LANES : (u + 1) * LANES]

    for i in range(1, cut + 1):
        if i < cut:
            xload(i).wait()
        for u in range(some):
            h = (i - 1) * some + u
            turn(h, h, 1, tiles)
        if i < cut:
            convolve_group(i)
        sum_main(i - 1)
        if i == 2:
            span_step(0)


    @pl.when(me > 0)
    def _():
        halo_copy.wait_recv()

    for j in range(width // LANES):
        edge[j, 0:8, :] = jnp.where(me == 0, 0.0, halo[:, lane(j)].astype(F32)[PACK - 8 :])
        edge[j, 8 : 8 + PACK, :] = xbc[0:PACK, lane(j)].astype(F32)
        done = activate(edge, j, 8, PACK, lane(j))
        if j < heads:
            v_first[0:PACK, lane(j)] = done
        else:
            maps[0:PACK, lane(j - heads)] = done

    def chunk(o):
        return (1 - side) * own + o if o < own else side * own + o - own

    def state(some):
        which = [start + chunk(o) for o in some for start in (theirs, mine)]
        base = 2 * some[0]
        for i, h in enumerate(which):
            turn(h, base + i, 0, 1)
        found = jnp.dot(
            dec[base * LANES : (base + len(which)) * LANES, 0:LANES], maps[0:LANES, lane(0)], preferred_element_type=F32
        )
        for i, h in enumerate(which):
            st = agg[h] + found[i * LANES : (i + 1) * LANES]
            agg[h] = st
            send[0, h] = st.astype(BF16)

    def part(start, o, n):
        if n == half:
            return pl.ds(start, half)
        return pl.ds(start + chunk(o), n)

    def side_of(o):
        return 1 - side if o < own else side

    def to_theirs(o, n=1):
        at = part(theirs, o, n)
        return remote(send.at[0, at], node.at[0, at], chip_send.at[0], chip_recv.at[side_of(o)], mate(0))

    def from_mate(o):
        at = part(mine, o, own)
        return remote(send.at[0, at], node.at[0, at], chip_send.at[0], chip_recv.at[side_of(o)], mate(0))

    def to_mine(o, n=1, start=mine):
        at = part(start, o, n)
        return remote(send.at[0, at], node.at[0, at], chip_send.at[1], chip_recv.at[2 + side_of(o)], mate(0))

    def step_copy(k, o, n=1):
        at = part(mine, o, n)
        if k == 1:
            s, r = step_send.at[o // own], step_recv.at[0 if n > 1 else chunk(o)]
        else:
            s, r = step_send.at[k], step_recv.at[half + (k - 2) * own + o - own]
        return remote(send.at[k, at], node.at[k, at], s, r, mate(k))

    def last_copy(o, hops=1, n=1, source=send):
        at = part(mine, o, n)
        to = lax.rem(me + hops * reach, count)
        return remote(source.at[last, at], node.at[last, at], last_send.at[hops - 1], last_recv.at[o - own], to)

    passed = own // 2

    def last_start(o):
        if o >= own + passed:
            last_copy(o, 2).start()
        last_copy(o).start()

    def x_forward(k, o, n=1):
        at = part(mine, o, n)
        return remote(node.at[k, at], node.at[k, at], xf_send.at[k - 2], xf_recv.at[(k - 2) * own + o % own], mate(1))

    def c_forward(k, o, n=1, start=mine):
        at = part(start, o, n)
        return remote(node.at[k, at], node.at[k, at], cf_send.at[k - 1], cf_recv.at[2 * (k - 1) + side_of(o)], mate(0))

    def combine(k, c):
        h = mine + c
        joined = agg[h] * factor[0, k, pl.ds(h, 1), :] + node[k, h].astype(F32) * factor[1, k, pl.ds(h, 1), :]
        agg[h] = joined
        send[k + 1, h] = joined.astype(BF16)

    def both_ways(k):
        return k < last - 1

    def sends(k, go):
        if both_ways(k):
            go()
        else:
            pl.when(bit_at(k) == 0)(go)

    def join_chip(which):
        from_mate(which[0]).wait_recv()
        for o in which:
            combine(0, chunk(o))
        if which[0] < own:
            for o in which:
                step_copy(1, o).start()
        else:
            @pl.when(side == 0)
            def _():
                for o in which:
                    step_copy(1, o).start()

    def join_x(o):
        step_copy(1, o).wait_recv()

        @pl.when(side == 1)
        def _():
            c_forward(1, o).start()

        combine(1, chunk(o))
        if last == 2:
            @pl.when(quarter == 1)
            def _():
                last_start(o)
        else:
            sends(2, lambda: step_copy(2, o).start())

    def take_x(o):
        @pl.when(side == 1)
        def _():
            step_copy(1, o).wait_recv()
            c_forward(1, o).start()

    def join(k, o):
        if both_ways(k):
            step_copy(k, o).wait_recv()

        @pl.when(bit_at(k) == 1)
        def _():
            if not both_ways(k):
                step_copy(k, o).wait_recv()
            x_forward(k, o).start()
            c_forward(k, o).start()

        if k + 1 < last:
            combine(k, chunk(o))
            sends(k + 1, lambda: step_copy(k + 1, o).start())
        else:
            @pl.when(quarter == 1)
            def _():
                combine(k, chunk(o))
                last_start(o)

    def take(k, o):
        @pl.when(bit_at(k) == 1)
        def _():
            x_forward(k, o).wait_recv()
            c_forward(k, o).start()

    def share_last(o):
        last_copy(o).wait_recv()
        x_forward(last, o).start()
        c_forward(last, o).start()

    def join_last():
        direct = range(own + passed, half)

        @pl.when(quarter == 2)
        def _():
            for o in range(own, own + passed):
                last_copy(o).wait_recv()
                last_copy(o, source=node).start()
                x_forward(last, o).start()
                c_forward(last, o).start()
            for o in direct:
                share_last(o)

        @pl.when(quarter == 3)
        def _():
            for o in direct:
                share_last(o)
            for o in range(own, own + passed):
                share_last(o)

    for some_heads in (range(own), range(own, half)):
        for o in some_heads[::2]:
            state((o, o + 1))
        for o in some_heads:
            to_theirs(o).start()

    @pl.when(core == 0)
    def _():
        for o in range(half):
            to_mine(o).start()

    join_chip(range(own))
    join_chip(range(own, half))

    late[0].wait()
    late[1].wait()
    lows = []
    for a in range(tiles):
        low = jnp.exp(ll[a] - mids[a])
        for l in range(tile_bits + 1):
            diag[l, :, lane(a)] = lw[l, :, lane(a)] * low
        for b in range(a):
            level = tile_bits + (a ^ b).bit_length()
            cross[a * (a - 1) // 2 + b] = lw[level, :, lane(a)] * jnp.exp(ll[a] - mids[b])
    out_map_t[...] = jnp.transpose(maps[:, lane(1)])
    s_all = lax.broadcasted_iota(jnp.int32, (LANES, LANES), 0)
    t_all = lax.broadcasted_iota(jnp.int32, (LANES, LANES), 1)
    for b in range(tiles):
        scored = jnp.dot(maps[lane(b), lane(0)], out_map_t[...], preferred_element_type=F32)
        for a in range(b, tiles):
            piece = scored[:, a * LANES : (a + 1) * LANES]
            scores_t[lane(b), lane(a)] = (jnp.where(s_all <= t_all, piece, 0.0) if a == b else piece).astype(BF16)
    flipped_gain = jnp.transpose(jnp.concatenate([gain[...], jnp.zeros((LANES - heads, LANES), F32)], axis=0))
    for h in range(heads):
        gain_col[h] = jnp.broadcast_to(flipped_gain[:, h : h + 1], (LANES, LANES))

    def far_table(k):
        level = local_bits + 1 + k
        for a in range(tiles):
            factor = lw[level, :, lane(a)] * jnp.exp(ll[a] + prefix[k])
            far_row[k, :, lane(a)] = jnp.where(bit_at(k) == 1, factor, 0.0)

    t_in = lax.broadcasted_iota(jnp.int32, (PACK, LANES), 1)
    s_in = lax.broadcasted_iota(jnp.int32, (PACK, LANES), 0)
    fine_bits = PACK.bit_length() - 1
    differ = jnp.bitwise_xor(s_in, jnp.bitwise_and(t_in, PACK - 1))
    t_group = lax.shift_right_logical(t_in, fine_bits)
    groups16 = LANES // PACK
    for u in range(wt.shape[0]):
        for a in range(0, tiles, 2):
            wt[u, lane(a + 1), lane(a)] = jnp.zeros((LANES, LANES), BF16)

    def spread(k, h, u):
        row = packed(far_row[k, pl.ds(h, 1), :])
        for s in range(groups16):
            at = k * LANES + s * PACK
            fw[u, at : at + PACK, :] = out_map_t[s * PACK : (s + 1) * PACK, :] * row

    def weights(h, u):
        for a in range(tiles):
            row = [diag[l, pl.ds(h, 1), lane(a)] for l in range(tile_bits + 1)]
            fine = row[fine_bits]
            for l in range(fine_bits - 1, 0, -1):
                fine = jnp.where(differ < (1 << l), row[l], fine)
            fine = jnp.where(differ == 0, row[0], fine).astype(BF16)
            wide = [packed(r) for r in row[fine_bits + 1 :]]
            for j in range(groups16):
                apart = jnp.bitwise_xor(t_group, j)
                chosen = fine
                for l in range(len(wide)):
                    if any((1 << l) <= (x ^ j) < (2 << l) for x in range(j, groups16)):
                        chosen = jnp.where((apart >= (1 << l)) & (apart < (2 << l)), wide[l], chosen)
                at = a * LANES + j * PACK
                wt[u, at : at + PACK, lane(a)] = chosen * scores_t[at : at + PACK, lane(a)]
            for b in range(a):
                row = packed(cross[a * (a - 1) // 2 + b, pl.ds(h, 1), :])
                for j in range(groups16):
                    at = b * LANES + j * PACK
                    wt[u, at : at + PACK, lane(a)] = row * scores_t[at : at + PACK, lane(a)]

    def held(k, h):
        source = node[k, h]
        return jnp.where(bit_at(k) == 1, source, jnp.zeros_like(source))

    def near(first, n):
        for u in range(n):
            weights(first + u, u)
        for u in range(n):
            h = first + u
            for a in range(0, tiles, 2):
                deep = (a + 2) * LANES
                near_t[h, :, a * LANES : deep] = jnp.dot(
                    values_t[h, :, 0:deep], wt[u, 0:deep, a * LANES : deep], preferred_element_type=F32
                )

    def far(h, u, low, high):
        left = jnp.concatenate([held(k, h) for k in range(low, high)], axis=1)
        return jnp.dot(left, fw[u, low * LANES : high * LANES, :], preferred_element_type=F32)

    def add_lower(first, n):
        for u in range(n):
            for k in range(last):
                spread(k, first + u, u)
        for u in range(n):
            near_t[first + u] += far(first + u, u, 0, last)

    def finish(first, n):
        for u in range(n):
            spread(last, first + u, u)
        for u in range(n):
            h = first + u
            mixed = near_t[h] + far(h, u, last, seq_bits)
            mean = jnp.mean(mixed * mixed, axis=0, keepdims=True)
            scaled = mixed * lax.rsqrt(mean + 1e-05) * jnp.concatenate([gain_col[h]] * tiles, axis=1)
            out[:, lane(h)] = jnp.transpose(scaled.astype(BF16))

    def finish_mine(o):
        finish(mine + chunk(o), own)

    def lower_mine(o):
        add_lower(mine + chunk(o), own)

    def lower_theirs(o):
        @pl.when(core == 1)
        def _():
            to_mine(o, own, theirs).wait_recv()

        for k in range(1, last):
            @pl.when(bit_at(k) == 1)
            def _():
                c_forward(k, o, own, theirs).wait_recv()

        add_lower(theirs + chunk(o), own)

    def finish_theirs(o):
        @pl.when(quarter >= 2)
        def _():
            c_forward(last, o, own, theirs).wait_recv()

        finish(theirs + chunk(o), own)

    def take_last(o):
        x_forward(last, o).wait_recv()
        c_forward(last, o).start()

    batch = wt.shape[0]
    far_table(0)
    far_table(1)
    other, kept = range(own), range(own, half)
    near(0, batch)
    near(batch, batch)
    span_step(1)
    for o in kept:
        join_x(o)
    near(2 * batch, batch)
    if last > 2:
        span_step(2)
    for k in range(2, last):
        if k > 2:
            span_step(k)
        far_table(k)
        for o in kept:
            join(k, o)
        if k == 2:
            for o in other:
                take_x(o)
            near(3 * batch, batch)
        if k < last - 1:
            for o in other:
                take(k, o)
    far_table(last)
    lower_mine(own)
    lower_theirs(own)
    join_last()
    if last > 2:
        for o in other:
            take(last - 1, o)
    lower_mine(0)
    lower_theirs(0)
    finish_mine(own)
    finish_theirs(own)
    @pl.when(quarter == 2)
    def _():
        for o in other:
            take_last(o)

    @pl.when(quarter == 3)
    def _():
        for o in [*other[passed:], *other[:passed]]:
            take_last(o)

    finish_mine(0)
    finish_theirs(0)

    @pl.when(me < count - 1)
    def _():
        halo_copy.wait_send()

    for k in range(last):
        span_copy(k).wait_send()
    to_theirs(0, half).wait_send()
    step_copy(1, 0, own).wait_send()

    @pl.when(core == 0)
    def _():
        to_mine(0, half).wait_send()

    @pl.when(side == 0)
    def _():
        step_copy(1, own, own).wait_send()

    @pl.when(side == 1)
    def _():
        c_forward(1, 0, half).wait_send()

    for k in range(2, last):
        sends(k, lambda: step_copy(k, own, own).wait_send())

        @pl.when(bit_at(k) == 1)
        def _():
            x_forward(k, own, own).wait_send()
            c_forward(k, 0, half).wait_send()

    @pl.when(quarter == 1)
    def _():
        last_copy(own, 1, own).wait_send()
        last_copy(own + passed, 2, own - passed).wait_send()

    @pl.when(quarter == 2)
    def _():
        last_copy(own, 1, passed, node).wait_send()

    @pl.when(quarter >= 2)
    def _():
        x_forward(last, own, own).wait_send()
        c_forward(last, 0, half).wait_send()


def on_device(xbc, conv_weight, log_decay, level_weights, gain):
    rows, width = xbc.shape
    heads = log_decay.shape[0]
    inner = gain.shape[0]
    dim = inner // heads
    tiles = rows // LANES
    levels = level_weights.shape[1]
    seq_bits = lax.axis_size("seq").bit_length() - 1
    last = seq_bits - 1
    dma = pltpu.SemaphoreType.DMA
    hbm = pl.BlockSpec(memory_space=pltpu.HBM)
    square = (heads, dim, LANES)
    return pl.pallas_call(
        functools.partial(kernel, seq_bits),
        out_shape=pltpu.VMEM((rows, inner), BF16),
        in_specs=[hbm] * 5,
        out_specs=pl.BlockSpec(memory_space=pltpu.VMEM),
        scratch_shapes=[
            pltpu.VMEM((rows, width), BF16),
            pltpu.VMEM(conv_weight.shape, F32),
            pltpu.VMEM((heads, rows), F32),
            pltpu.VMEM((levels, heads, rows), F32),
            pltpu.VMEM((heads, dim), F32),
            dma((9,)),
            pltpu.VMEM((heads // 2, rows + 8, LANES), F32),
            pltpu.VMEM((width // LANES, PACK + 8, LANES), F32),
            pltpu.VMEM((PACK, width), BF16),
            pltpu.VMEM((LANES, inner), BF16),
            pltpu.VMEM((4, rows - LANES, inner // 4), BF16),
            pltpu.VMEM((rows, width - inner), BF16),
            pltpu.VMEM((LANES, rows), BF16),
            pltpu.VMEM((heads, dim, rows), BF16),
            pltpu.VMEM((heads * dim, rows), BF16),
            pltpu.VMEM((heads, rows), F32),
            pltpu.VMEM((heads, rows), F32),
            pltpu.VMEM((LANES.bit_length(), heads, rows), F32),
            pltpu.VMEM((tiles * (tiles - 1) // 2, heads, LANES), F32),
            pltpu.VMEM((seq_bits, heads, rows), F32),
            pltpu.VMEM((rows, rows), BF16),
            pltpu.VMEM((heads // 4, rows, rows), BF16),
            pltpu.VMEM((heads // 4, seq_bits * LANES, rows), BF16),
            pltpu.VMEM((heads, dim, rows), F32),
            pltpu.VMEM(square, F32),
            pltpu.VMEM(square, F32),
            pltpu.VMEM((seq_bits,) + square, BF16),
            pltpu.VMEM((seq_bits,) + square, BF16),
            pltpu.VMEM((seq_bits + 1, heads, LANES), F32),
            pltpu.VMEM((seq_bits, heads, LANES), F32),
            pltpu.VMEM((seq_bits + 1, heads, LANES), F32),
            pltpu.VMEM((2, seq_bits, heads, LANES), F32),
            dma((2,)),
            dma((last,)),
            dma((last,)),
            dma((2,)),
            dma((4,)),
            dma((last,)),
            dma((heads // 2 + (last - 2) * heads // 4,)),
            dma((2,)),
            dma((heads // 4,)),
            dma((last - 1,)),
            dma(((last - 1) * heads // 4,)),
            dma((last,)),
            dma((2 * last,)),
        ],
        compiler_params=pltpu.CompilerParams(
            collective_id=0, has_side_effects=True, vmem_limit_bytes=61 * 1024 * 1024
        ),
        name="mixer",
    )(xbc, conv_weight, log_decay, level_weights.transpose(1, 0, 2), gain.reshape(heads, dim))


def solution(mesh):
    in_specs = (
        P(("groups", "seq"), None),
        P(),
        P(None, ("groups", "seq")),
        P(None, None, ("groups", "seq")),
        P(),
    )
    out_specs = P(("groups", "seq"), None)
    return jax.shard_map(
        on_device, mesh=mesh, in_specs=in_specs, out_specs=out_specs, check_vma=False
    )
```
